32 devices in a mesh: circ: 8 (over z, x), cell: 4 (over y, core).
Axes of the slice: x: 2, y: 2, z: 4, core: 2. Of those that a mesh axis runs over, the one named last changes fastest.
Arguments:
- flow_state: bfloat16 [35, 8, 16, 1024], P(None, 'circ', 'cell'), may hold values from -6 to 6
- time_coef: float32 [8, 16, 1024], P('circ', 'cell'), may hold values from 0.3 to 3
- axial_damp: bfloat16 [8, 16, 1024], P('circ', 'cell'), may hold values from 0.19921875 to 2
- plane_damp: bfloat16 [8, 16, 2048], P('circ', 'cell'), may hold values from 0.19921875 to 2
- periodic_damp: bfloat16 [8, 16, 64], P('circ', 'cell'), may hold values from 0.19921875 to 2
- flux_jacobian: float32 [3, 5, 5], replicated, may hold values from -2.5 to 2.5
- face_cells: int32 [2, 2048], replicated, may hold values from 0 to 1023, as said below
- periodic_cells: int32 [2, 64], replicated, may hold values from 0 to 1023, as said below
- face_map: int32 [64], replicated, may hold values from 0 to 63, each once
- wall_cells: int32 [1024], P('cell'), may hold values from 0 to 4095, as said below
- wall_normals: float32 [3, 1024], P(None, 'cell'), may hold values from -6 to 6
- pressure_weights: float32 [5], replicated, may hold values from -4 to 4
- mode_shapes: float32 [2, 8, 3, 400], replicated, may hold values from -0.00390625 to 0.00390625
Outputs:
- jacobian_image: bfloat16 [35, 8, 16, 1024], P(None, 'circ', 'cell')
- modal_forces: float32 [7, 400], replicated
The draws below stay inside these ranges and needn't reach their ends.
Inputs may be any that keep to these rules, and one draw needn't show every extreme that they name: `face_cells`: each column names the two cells of a layer that one in-plane face joins; the two differ. `periodic_cells`: all 128 entries differ. `face_map`: each value of 0 to 63 once. `wall_cells`: an entry is the wall cell's layer within its cell block times 1024 plus its cell in the layer; entries may repeat.
All inputs are finite; a program needn't handle non-finite values.
Results may differ from the reference program's by a relative error of at most 0.0055.
Values may be sent and summed in bfloat16 or wider, within the bound.
A program may use at most 64 MiB of HBM per device.

```python
import math
import jax
import jax.numpy as jnp
import numpy as np
from jax import lax

NV = 5
HB = 7
PLANE = 1024
AX_DEV = 4
PER = 64
WALL_DEV = 256
MODES = 400
AXIAL = 16
FACES = 2048
WALLS = 1024
PASSAGES = 8


def draw_face_cells(key, part):
    key_near = jax.random.fold_in(key, 11)
    key_far = jax.random.fold_in(key, 12)
    key_order = jax.random.fold_in(key, 13)
    cell_ids = jnp.arange(PLANE, dtype=jnp.int32)
    near_step = jax.random.randint(key_near, (PLANE,), 1, 4)
    far_step = jax.random.randint(key_far, (PLANE,), 15, 19)
    owners = jnp.concatenate([cell_ids, cell_ids])
    neighbours = jnp.concatenate([(cell_ids + near_step) % PLANE, (cell_ids + far_step) % PLANE])
    face_order = jax.random.permutation(key_order, 2 * PLANE)
    joined_pairs = jnp.stack([owners, neighbours])[:, face_order]
    return joined_pairs.astype(jnp.int32)


def draw_periodic_cells(key, part):
    key_pick = jax.random.fold_in(key, 21)
    key_order = jax.random.fold_in(key, 22)
    inner_cells = jax.random.permutation(key_pick, PLANE - 2)[:2 * PER - 2] + 1
    chosen = jnp.concatenate([jnp.array([0, PLANE - 1], jnp.int32), inner_cells.astype(jnp.int32)])
    chosen = chosen[jax.random.permutation(key_order, 2 * PER)]
    return chosen.reshape(2, PER).astype(jnp.int32)


def draw_wall_cells(key, part):
    key_values = jax.random.fold_in(key, 31)
    key_high = jax.random.fold_in(key, 32)
    key_low = jax.random.fold_in(key, 33)
    limit = AX_DEV * PLANE
    wall_values = jax.random.randint(key_values, (WALLS,), 0, limit)
    high_spot = jax.random.randint(key_high, (), 0, WALLS)
    low_spot = (high_spot + 1 + jax.random.randint(key_low, (), 0, WALLS - 1)) % WALLS
    positions = jnp.arange(WALLS, dtype=jnp.int32)
    wall_values = jnp.where(positions == high_spot, limit - 1, wall_values)
    wall_values = jnp.where(positions == low_spot, 0, wall_values)
    return wall_values.astype(jnp.int32)


def level_of(rng, shape, cuts, smallest, top_value):
    level, own = 1.0, jax.random.fold_in(rng, 6)
    for position, shards_of in cuts:
        steps = jnp.exp(jax.random.uniform(jax.random.fold_in(own, position), (shards_of,), jnp.float32, smallest / len(cuts), top_value / len(cuts)))
        level = level * jnp.repeat(steps, shape[position] // shards_of).reshape([-1 if axis == position else 1 for axis in range(len(shape))])
    return level


def scatter_about(stream_key, extent, width, reach, pieces=(), kind=jnp.bfloat16):
    factor_of = level_of(stream_key, extent, pieces, -0.22, 0.18) if pieces else 1.0
    values = jax.random.normal(stream_key, extent, jnp.float32) * width * factor_of
    return jnp.minimum(jnp.maximum(values, -reach), reach).astype(kind)


def setup_inputs(seed: int = 0) -> dict:
    key_list = jax.random.split(jax.random.key(seed), 14)
    return {
        "flow_state": scatter_about(key_list[0], (HB * NV, PASSAGES, AXIAL, PLANE), 1.0, 6.0, ((1, 8), (2, 4))),
        "time_coef": jnp.clip(jnp.exp(math.log(3.0) - 2.3025851 * jax.random.uniform(key_list[1], (PASSAGES, AXIAL, PLANE), jnp.float32) ** level_of(key_list[1], (PASSAGES, AXIAL, PLANE), ((0, 8), (1, 4)), -0.2, 0.2)), 0.3, 3.0),
        "axial_damp": jnp.clip(jnp.exp(math.log(2.0) - 2.306499 * jax.random.uniform(key_list[2], (PASSAGES, AXIAL, PLANE), jnp.float32) ** level_of(key_list[2], (PASSAGES, AXIAL, PLANE), ((0, 8), (1, 4)), -0.2, 0.2)), 0.19921875, 2.0).astype(jnp.bfloat16),
        "plane_damp": jnp.clip(jnp.exp(math.log(2.0) - 2.306499 * jax.random.uniform(key_list[3], (PASSAGES, AXIAL, FACES), jnp.float32) ** level_of(key_list[3], (PASSAGES, AXIAL, FACES), ((0, 8), (1, 4)), -0.2, 0.2)), 0.19921875, 2.0).astype(jnp.bfloat16),
        "periodic_damp": jnp.clip(jnp.exp(math.log(2.0) - 2.306499 * jax.random.uniform(key_list[4], (PASSAGES, AXIAL, PER), jnp.float32) ** level_of(key_list[4], (PASSAGES, AXIAL, PER), ((0, 8), (1, 4)), -0.2, 0.2)), 0.19921875, 2.0).astype(jnp.bfloat16),
        "flux_jacobian": scatter_about(key_list[5], (3, NV, NV), NV ** -0.5, 2.5, (), jnp.float32),
        "face_cells": draw_face_cells(jax.random.fold_in(key_list[13], 71), 0),
        "periodic_cells": draw_periodic_cells(jax.random.fold_in(key_list[13], 71), 0),
        "face_map": jax.random.permutation(key_list[8], PER).astype(jnp.int32),
        "wall_cells": draw_wall_cells(jax.random.fold_in(key_list[13], 71), 0),
        "wall_normals": scatter_about(key_list[10], (3, WALLS), 1.0, 6.0, ((1, 4),), jnp.float32),
        "pressure_weights": scatter_about(key_list[11], (NV,), 1.0, 4.0, (), jnp.float32),
        "mode_shapes": scatter_about(key_list[12], (2, PASSAGES, 3, MODES), (30 * WALLS * PASSAGES * PASSAGES) ** -0.5, 0.00390625, (), jnp.float32),
    }


def harmonic_matrix(instances):
    matrix_table = np.zeros((instances, instances))
    for row_index in range(instances):
        for column_index in range(instances):
            if row_index != column_index:
                offset_steps = row_index - column_index
                matrix_table[row_index, column_index] = 0.5 * (-1.0) ** offset_steps / math.sin(math.pi * offset_steps / instances)
    return matrix_table


def face_flux(jacobian, damping, lower_state, upper_state):
    total_state = lower_state + upper_state
    jump_state = upper_state - lower_state
    convected = jnp.einsum("vw,nw...->nv...", jacobian, total_state, precision=lax.Precision.HIGHEST)
    return 0.5 * convected - 0.5 * damping * jump_state


def reference(flow_state, time_coef, axial_damp, plane_damp, periodic_damp, flux_jacobian, face_cells, periodic_cells, face_map, wall_cells, wall_normals, pressure_weights, mode_shapes):
    state_all = flow_state.reshape(HB, NV, PASSAGES, AXIAL, PLANE)
    lower_side = periodic_cells[0]
    upper_side = periodic_cells[1]
    targets = lower_side[face_map]
    lower_values = state_all[..., lower_side].astype(jnp.float32)
    upper_values = state_all[..., upper_side].astype(jnp.float32)
    matched_next = jnp.roll(lower_values, -1, axis=2)[..., face_map]
    periodic_all = face_flux(flux_jacobian[2], periodic_damp.astype(jnp.float32), upper_values, matched_next)
    from_previous = jnp.roll(periodic_all, 1, axis=2)
    harmonic = jnp.asarray(harmonic_matrix(HB), jnp.float32)
    block_of_wall = jnp.arange(WALLS, dtype=jnp.int32) // WALL_DEV
    wall_layer = block_of_wall * AX_DEV + wall_cells // PLANE
    wall_column = wall_cells % PLANE
    owners = face_cells[0]
    neighbours = face_cells[1]

    def one_passage(passage_inputs):
        passage_state, cell_coef, damp_axial, damp_plane, own_periodic, incoming = passage_inputs
        current = passage_state.astype(jnp.float32)
        jacobian_sum = cell_coef[None, None] * jnp.einsum("nm,mvac->nvac", harmonic, current, precision=lax.Precision.HIGHEST)
        plane_flux = face_flux(flux_jacobian[1], damp_plane.astype(jnp.float32), current[..., owners], current[..., neighbours])
        jacobian_sum = jacobian_sum.at[..., owners].add(plane_flux).at[..., neighbours].add(-plane_flux)
        upper_rows = jnp.concatenate([current[:, :, 1:], jnp.zeros((HB, NV, 1, PLANE), jnp.float32)], axis=2)
        own_flux = face_flux(flux_jacobian[0], damp_axial.astype(jnp.float32), current, upper_rows)
        jacobian_sum = jacobian_sum + own_flux
        jacobian_sum = jacobian_sum.at[:, :, 1:].add(-own_flux[:, :, :-1])
        jacobian_sum = jacobian_sum.at[..., upper_side].add(own_periodic).at[..., targets].add(-incoming)
        wall_state = current[:, :, wall_layer, wall_column]
        wall_pressure = jnp.einsum("v,nvw->nw", pressure_weights, wall_state, precision=lax.Precision.HIGHEST)
        block_force = jnp.einsum("kw,nw->kn", wall_normals, wall_pressure, precision=lax.Precision.HIGHEST)
        return jacobian_sum.astype(jnp.bfloat16), block_force

    images, forces = lax.map(one_passage, (jnp.moveaxis(state_all, 2, 0), time_coef, axial_damp, plane_damp, jnp.moveaxis(periodic_all, 2, 0), jnp.moveaxis(from_previous, 2, 0)))
    jacobian_image = jnp.moveaxis(images, 0, 2).reshape(HB * NV, PASSAGES, AXIAL, PLANE)
    spectrum = jnp.fft.fft(forces, axis=0)
    real_part = jnp.real(spectrum)
    imag_part = jnp.imag(spectrum)
    modal_forces = jnp.einsum("dkm,dkn->nm", mode_shapes[0], real_part, precision=lax.Precision.HIGHEST) + jnp.einsum("dkm,dkn->nm", mode_shapes[1], imag_part, precision=lax.Precision.HIGHEST)
    return jacobian_image, modal_forces
```

```python
import functools
import math

import jax
import jax.numpy as jnp
import numpy as np
from jax import lax
from jax.experimental import pallas as pl
from jax.experimental.pallas import tpu as pltpu
from jax.sharding import PartitionSpec as P

NV = 5
HB = 7
F32 = jnp.float32
BF16 = jnp.bfloat16
F8 = jnp.float8_e4m3fn
GROUP = 32
HI = lax.Precision.HIGHEST
MESH = pl.DeviceIdType.MESH
NT = (((1,), (1,)), ((), ()))


def up_to(value, step):
    return -(-value // step) * step


def harmonic_matrix(instances):
    matrix = np.zeros((instances, instances))
    for n in range(instances):
        for m in range(instances):
            if n != m:
                matrix[n, m] = 0.5 * (-1.0) ** (n - m) / math.sin(math.pi * (n - m) / instances)
    return matrix


def near_scale(values):
    scales = 1.0 + np.arange(4096) / 4096.0
    scaled = scales[:, None] * values[None, :]
    rounded = scaled.astype(BF16).astype(np.float64)
    return float(scales[np.argmin(np.max(np.abs(rounded / scaled - 1.0), axis=1))])


def constants(layers, passages, walls_k):
    rows = HB * NV * layers
    padded = up_to(rows, 16)
    side = up_to(HB * NV, 16)
    width = padded + 2 * side
    harmonic = harmonic_matrix(HB)
    scale = near_scale(np.unique(np.abs(harmonic[harmonic != 0])))
    mix = np.zeros((padded, padded), np.float32)
    axial = np.zeros((padded, width), np.float32)
    fixed = np.zeros((3, padded, width), np.float32)
    pick = np.zeros((2 * side, padded), np.float32)
    weights = np.zeros((8, padded), np.int32)
    of_row = np.zeros((padded, NV), np.float32)
    of_column = np.zeros((NV, width), np.float32)
    for i in range(rows):
        r, a = divmod(i, layers)
        n, v = divmod(r, NV)
        of_row[i, v] = 1
        of_column[v, i] = 1
        of_column[v, padded + r] = 1
        of_column[v, padded + side + r] = 1
        weights[n, i] = v + 1
        if a == 0:
            pick[r, i] = 1
        if a == layers - 1:
            pick[side + r, i] = 1
        for w in range(NV):
            q = n * NV + w
            mix[i, q * layers + a] = 1
            axial[i, q * layers + a + 1 if a < layers - 1 else padded + q] = 1
            axial[i, q * layers + a - 1 if a > 0 else padded + side + q] = -1
        fixed[1, i, i] = -1
        fixed[1, i, i + 1 if a < layers - 1 else padded + r] = 1
        fixed[2, i, i] = -1
        fixed[2, i, i - 1 if a > 0 else padded + side + r] = 1
        for m in range(HB):
            fixed[0, i, (m * NV + v) * layers + a] = scale * harmonic[n, m]
    lanes = up_to(walls_k * passages, 128)
    modes = np.zeros((lanes, 2 * walls_k * passages), np.float32)
    for p in range(passages):
        for d in range(passages):
            angle = 2.0 * math.pi * (d * p % passages) / passages
            for k in range(walls_k):
                modes[p * walls_k + k, k * passages + d] = math.cos(angle)
                modes[p * walls_k + k, (walls_k + k) * passages + d] = -math.sin(angle)
    arrays = (
        mix,
        axial,
        fixed.reshape(3 * padded, width).astype(BF16),
        pick.astype(BF16),
        weights,
        of_row.astype(BF16),
        of_column.astype(BF16),
        modes,
    )
    return arrays, scale


def dot(a, b):
    return jnp.dot(a, b, preferred_element_type=F32)


def kernel(
    state, time_coef, axial_damp, plane_damp, periodic_damp, jac, faces, sides, face_map,
    wall_cells, normals, press_w, mode_shapes,
    mix_c, axial_c, fixed_c, pick_c, weights_c, of_row_c, of_column_c, modes_c,
    image, modal,
    extra, signed, joint, stack, cell_out, above, below, side_out, side_next, side_prev,
    forces_1, forces_2, flux, total,
    cell_send, cell_recv, side_send, side_recv, f1_send, f1_recv, f2_send, f2_recv,
    *, n_cell, n_circ, layers, padded, scale,
):
    me_cell = lax.axis_index("cell")
    me_circ = lax.axis_index("circ")

    def cell_at(j):
        return {"cell": lax.rem(me_cell + j, n_cell)}

    def circ_at(j):
        return {"circ": lax.rem(me_circ + j, n_circ)}

    barrier = pltpu.get_barrier_semaphore()
    for j in range(1, n_cell):
        pl.semaphore_signal(barrier, inc=1, device_id=cell_at(j), device_id_type=MESH)
    for j in range(1, n_circ):
        pl.semaphore_signal(barrier, inc=1, device_id=circ_at(j), device_id_type=MESH)

    n_rows, _, cells = state.shape
    n_faces = faces.shape[1]
    n_walls = wall_cells.shape[1]
    per = sides.shape[1]
    side_rows = above.shape[0]
    walls_k = normals.shape[0]
    groups = padded // 8

    def by_layer(value, pattern):
        return (value.reshape(groups, 8, value.shape[1]) * pattern[None]).reshape(value.shape)

    def pattern_of(rows):
        return jnp.concatenate([rows] * (8 // layers), axis=0)

    wide = state[...].astype(F32)
    pieces = [wide[r] for r in range(n_rows)]
    pieces.append(jnp.zeros((padded - n_rows * layers, cells), F32))
    u = jnp.concatenate(pieces, axis=0).astype(BF16)

    order = face_map[...]
    hits = (lax.broadcasted_iota(jnp.int32, (per, per), 0) == order).astype(F32)
    targets = jnp.dot(sides[0:1, :].astype(F32), hits, precision=HI, preferred_element_type=F32)
    targets = (targets + 0.5).astype(jnp.int32)
    wall_index = wall_cells[...]
    wall_layer = lax.div(wall_index, cells)
    wall_column = wall_index - wall_layer * cells
    columns = jnp.concatenate([wall_column, sides[1:2, :], targets], axis=1)
    band = lax.broadcasted_iota(jnp.int32, (GROUP, 128), 0).astype(F32).astype(BF16)
    one = jnp.ones((GROUP, 128), BF16)
    zero = jnp.zeros((GROUP, 128), BF16)

    def spread(row):
        return jnp.broadcast_to(row.astype(F32).astype(BF16), (GROUP, 128))

    def split(row):
        high = lax.shift_right_logical(row, GROUP.bit_length() - 1)
        return spread(high), jnp.where(band == spread(row - high * GROUP), one, zero)

    for at in range(0, extra.shape[1], 128):
        high, low = split(columns[:, at : at + 128])
        for h in range(cells // GROUP):
            hit = jnp.where(high == h, low, zero)
            extra[h * GROUP : (h + 1) * GROUP, at : at + 128] = hit.astype(F8)

    cell_out[0 : 2 * side_rows, :] = dot(pick_c[...], u).astype(BF16)
    damp = axial_damp[0].astype(F32)
    last = damp[layers - 1 : layers]
    cell_out[2 * side_rows :, :] = jnp.broadcast_to(last, (16, cells)).astype(BF16)

    gathered = dot(u, extra[...])
    own_side = gathered[:, n_walls:]
    side_out[0:padded, :] = own_side.astype(BF16)
    side_damp = periodic_damp[0].astype(F32)
    side_pattern = pattern_of(jnp.concatenate([side_damp, side_damp], axis=1))
    side_out[padded:, :] = jnp.concatenate([side_pattern, side_pattern], axis=0).astype(BF16)

    layer_of = lax.rem(lax.broadcasted_iota(jnp.int32, (8, n_walls), 0), layers)
    here = by_layer(gathered[:, :n_walls], (layer_of == wall_layer).astype(F32))
    weight_class = weights_c[...]
    weight = jnp.zeros(weight_class.shape, F32)
    for v in range(NV):
        weight = jnp.where(weight_class == v + 1, press_w[v], weight)
    pressure = jnp.dot(weight, here, precision=HI, preferred_element_type=F32)
    force = lax.dot_general(pressure, normals[...], NT, precision=HI, preferred_element_type=F32)
    lanes = forces_1.shape[2]
    lane = lax.broadcasted_iota(jnp.int32, (8, lanes), 1)
    tile = jnp.zeros((8, lanes), F32)
    for k in range(walls_k):
        tile = jnp.where(lane == me_circ * walls_k + k, force[:, k : k + 1], tile)
    forces_1[me_cell] = tile

    def mixing(face, mask):
        values = (0.5 * jac[:, face, :]).astype(BF16)
        across = dot(values, of_column_c[:, : mask.shape[1]]).astype(BF16)
        return (dot(of_row_c[...], across) * mask).astype(BF16)

    axial_mix = mixing(0, axial_c[...])
    plane_mix = mixing(1, mix_c[...])
    side_mix = mixing(2, mix_c[...])

    convected = dot(plane_mix, u).astype(BF16)
    plane_pattern = pattern_of(0.5 * plane_damp[0].astype(F32))

    def build(first, count):
        for at in range(first, first + count, 128):
            owner_high, owner = split(faces[0:1, at : at + 128])
            other_high, other = split(faces[1:2, at : at + 128])
            same = owner_high == other_high
            both = owner - other
            by_owner = jnp.where(same, both, owner)
            by_other = jnp.where(same, both, -other)
            for h in range(cells // GROUP):
                hit = jnp.where(other_high == h, by_other, zero)
                hit = jnp.where(owner_high == h, by_owner, hit)
                here = slice(h * GROUP, (h + 1) * GROUP)
                signed[here, at : at + 128] = hit.astype(F8)
                joint[here, at : at + 128] = jnp.abs(hit).astype(F8)

    def gather(first, count):
        here = slice(first, first + count)
        damped = by_layer(dot(u, signed[:, here]), plane_pattern[:, here])
        flux[:, here] = (dot(convected, joint[:, here]) + damped).astype(BF16)

    part = 256
    starts = list(range(0, n_faces, part))
    early = len(starts) // 4
    build(0, part)
    for at in starts[:early]:
        build(at + part, part)
        gather(at, part)

    pl.semaphore_wait(barrier, n_cell - 1 + n_circ - 1)
    copies = []

    def send(source, target, send_sem, recv_sem, device):
        copy = pltpu.make_async_remote_copy(
            src_ref=source, dst_ref=target, send_sem=send_sem, recv_sem=recv_sem,
            device_id=device, device_id_type=MESH,
        )
        copy.start()
        copies.append(copy)
        return copy

    to_below = send(
        cell_out.at[pl.ds(0, side_rows)], above, cell_send.at[0], cell_recv.at[0],
        cell_at(n_cell - 1),
    )
    to_above = send(
        cell_out.at[pl.ds(side_rows, side_rows + 16)], below, cell_send.at[1], cell_recv.at[1],
        cell_at(1),
    )
    to_prev = send(side_out, side_next, side_send.at[0], side_recv.at[0], circ_at(n_circ - 1))
    to_next = send(side_out, side_prev, side_send.at[1], side_recv.at[1], circ_at(1))
    first = [
        send(forces_1.at[me_cell], forces_1.at[me_cell], f1_send.at[j], f1_recv.at[j], cell_at(j))
        for j in range(1, n_cell)
    ]

    def chunks(some):
        for at in some:
            if at + part < n_faces:
                build(at + part, part)
            gather(at, part)

    joined = len(starts) // 2
    chunks(starts[early:joined])
    for copy in first:
        copy.wait_recv()
    summed = forces_1[0]
    for j in range(1, n_cell):
        summed = summed + forces_1[j]
    forces_2[0] = summed
    chunks(starts[joined : joined + 1])
    second = [
        send(forces_2.at[0], forces_2.at[j], f2_send.at[j], f2_recv.at[j], circ_at(j))
        for j in range(1, n_circ)
    ]
    chunks(starts[joined + 1 :])
    shapes = mode_shapes[...].reshape(2 * walls_k * n_circ, mode_shapes.shape[3])
    by_passage = jnp.dot(modes_c[...], shapes, precision=HI, preferred_element_type=F32)

    total[...] = lax.dot_general(
        flux[...], signed[...], NT, preferred_element_type=F32
    )

    to_below.wait_recv()
    to_above.wait_recv()
    stack[0:padded, :] = u
    above_rows = above[...].astype(F32)
    stack[padded : padded + side_rows, :] = jnp.where(
        me_cell == n_cell - 1, 0.0, above_rows
    ).astype(BF16)
    below_rows = below[0:side_rows, :].astype(F32)
    stack[padded + side_rows :, :] = jnp.where(
        me_cell == 0, -cell_out[0:side_rows, :].astype(F32), below_rows
    ).astype(BF16)
    below_damp = below[side_rows : side_rows + 16, :].astype(F32)[0:1]
    below_damp = jnp.where(me_cell == 0, 0.0, below_damp)
    held = stack[...]
    derived = dot(fixed_c[...], held)
    result = by_layer(derived[0:padded], pattern_of(time_coef[0] * (1.0 / scale)))
    result = result - by_layer(derived[padded : 2 * padded], pattern_of(0.5 * damp))
    lower_damp = jnp.concatenate([below_damp, damp[0 : layers - 1]], axis=0)
    result = result - by_layer(derived[2 * padded :], pattern_of(0.5 * lower_damp))
    result = result + dot(axial_mix, held)

    to_prev.wait_recv()
    to_next.wait_recv()
    left = lax.broadcasted_iota(jnp.int32, (padded, 2 * per), 1) < per
    ahead = pltpu.roll(side_next[0:padded, :].astype(F32), per, 1)
    back = pltpu.roll(side_prev[0:padded, :].astype(F32), per, 1)
    back_damp = side_prev[padded:, :].astype(F32)[0:8]
    lower = jnp.where(left, own_side, back)
    upper = jnp.where(left, ahead, own_side)
    side_s = 0.5 * jnp.where(left[0:8], side_pattern, back_damp)
    lower_b, upper_b = lower.astype(BF16), upper.astype(BF16)
    side_flux = dot(side_mix, lower_b) + dot(side_mix, upper_b)
    side_flux = side_flux - by_layer(upper - lower, side_s)
    side_flux = jnp.where(left, side_flux, -side_flux).astype(BF16)
    result = result + lax.dot_general(
        side_flux, extra[:, n_walls:], NT, preferred_element_type=F32
    )
    result = result + total[...]
    for r in range(n_rows):
        image[r] = result[r * layers : (r + 1) * layers].astype(BF16)

    for copy in second:
        copy.wait_recv()
    every = forces_2[0]
    for j in range(1, n_circ):
        every = every + forces_2[j]
    answer = jnp.dot(every, by_passage, precision=HI, preferred_element_type=F32)
    modal[...] = answer[0:HB]
    for copy in copies:
        copy.wait_send()


def deliver(image, modal, image_out, modal_out, sems):
    copies = [
        pltpu.make_async_copy(image, image_out, sems.at[0]),
        pltpu.make_async_copy(modal, modal_out, sems.at[1]),
    ]
    for copy in copies:
        copy.start()
    for copy in copies:
        copy.wait()


def shards(
    flow_state, time_coef, axial_damp, plane_damp, periodic_damp, flux_jacobian, face_cells,
    periodic_cells, face_map, wall_cells, wall_normals, pressure_weights, mode_shapes,
):
    layers, cells = flow_state.shape[2:]
    n_cell = lax.axis_size("cell")
    n_circ = lax.axis_size("circ")
    walls_k = wall_normals.shape[0]
    n_modes = mode_shapes.shape[3]
    per = face_map.shape[0]
    n_faces = face_cells.shape[1]
    n_walls = wall_cells.shape[0]
    fixed, scale = constants(layers, n_circ, walls_k)
    padded = fixed[0].shape[0]
    side = fixed[3].shape[0] // 2
    lanes = fixed[7].shape[0]
    state = flow_state.reshape(HB * NV, layers, cells)
    vmem = pl.BlockSpec(memory_space=pltpu.VMEM)
    smem = pl.BlockSpec(memory_space=pltpu.SMEM)
    dma = pltpu.SemaphoreType.DMA
    image, modal = pl.pallas_call(
        functools.partial(
            kernel, n_cell=n_cell, n_circ=n_circ, layers=layers, padded=padded, scale=scale
        ),
        out_shape=(
            jax.ShapeDtypeStruct((HB * NV, layers, cells), BF16),
            jax.ShapeDtypeStruct((HB, n_modes), F32),
        ),
        in_specs=[vmem] * 11 + [smem] + [vmem] * 9,
        out_specs=(vmem, vmem),
        scratch_shapes=[
            pltpu.VMEM((cells, n_walls + 2 * per), F8),
            pltpu.VMEM((cells, n_faces), F8),
            pltpu.VMEM((cells, n_faces), F8),
            pltpu.VMEM((padded + 2 * side, cells), BF16),
            pltpu.VMEM((2 * side + 16, cells), BF16),
            pltpu.VMEM((side, cells), BF16),
            pltpu.VMEM((side + 16, cells), BF16),
            pltpu.VMEM((padded + 16, 2 * per), BF16),
            pltpu.VMEM((padded + 16, 2 * per), BF16),
            pltpu.VMEM((padded + 16, 2 * per), BF16),
            pltpu.VMEM((n_cell, 8, lanes), F32),
            pltpu.VMEM((n_circ, 8, lanes), F32),
            pltpu.VMEM((padded, n_faces), BF16),
            pltpu.VMEM((padded, cells), F32),
            dma((2,)), dma((2,)), dma((2,)), dma((2,)),
            dma((n_cell,)), dma((n_cell,)), dma((n_circ,)), dma((n_circ,)),
        ],
        compiler_params=pltpu.CompilerParams(collective_id=0, has_side_effects=True),
    )(
        state, time_coef, axial_damp, plane_damp, periodic_damp,
        flux_jacobian.transpose(1, 0, 2), face_cells, periodic_cells, face_map[None], wall_cells[None], wall_normals, pressure_weights,
        mode_shapes.transpose(0, 2, 1, 3), *fixed,
    )
    anywhere = pl.BlockSpec(memory_space=pl.ANY)
    image, modal = pl.pallas_call(
        deliver,
        out_shape=(
            jax.ShapeDtypeStruct(image.shape, BF16),
            jax.ShapeDtypeStruct(modal.shape, F32),
        ),
        in_specs=[anywhere] * 2,
        out_specs=(vmem, vmem),
        scratch_shapes=[dma((2,))],
    )(image, modal)
    return image.reshape(HB * NV, 1, layers, cells), modal


def solution(mesh):
    circ = P("circ", "cell", None)
    placed = (
        P(None, "circ", "cell", None), circ, circ, circ, circ, P(), P(), P(), P(),
        P("cell"), P(None, "cell"), P(), P(),
    )
    return jax.shard_map(
        shards,
        mesh=mesh,
        in_specs=placed,
        out_specs=(P(None, "circ", "cell", None), P()),
        check_vma=False,
    )
```

```python
import functools
import math

import jax
import jax.numpy as jnp
import numpy as np
from jax import lax
from jax.experimental import pallas as pl
from jax.experimental.pallas import tpu as pltpu
from jax.sharding import PartitionSpec as P

NV = 5
HB = 7
F32 = jnp.float32
BF16 = jnp.bfloat16
F8 = jnp.float8_e4m3fn
GROUP = 32
VMEM_LIMIT = 24 << 20
(
    STATE, TIME_COEF, AXIAL_DAMP, PLANE_DAMP, PERIODIC_DAMP, JAC, FACES, SIDES, FACE_MAP,
    WALL_CELLS, NORMALS, PRESS_W, MODE_SHAPES,
    MIX_C, AXIAL_C, FIXED_C, PICK_C, WEIGHTS_C, OF_ROW_C, OF_COLUMN_C, MODES_C,
) = range(21)
LOAD_ORDER = (
    STATE, WALL_CELLS, NORMALS, PRESS_W, WEIGHTS_C, FACE_MAP, SIDES, PERIODIC_DAMP, AXIAL_DAMP,
    PICK_C, JAC, OF_ROW_C, OF_COLUMN_C, MIX_C, AXIAL_C, PLANE_DAMP, FACES, MODE_SHAPES, MODES_C,
    FIXED_C, TIME_COEF,
)
HI = lax.Precision.HIGHEST
MESH = pl.DeviceIdType.MESH
NT = (((1,), (1,)), ((), ()))


def up_to(value, step):
    return -(-value // step) * step


def harmonic_matrix(instances):
    matrix = np.zeros((instances, instances))
    for n in range(instances):
        for m in range(instances):
            if n != m:
                matrix[n, m] = 0.5 * (-1.0) ** (n - m) / math.sin(math.pi * (n - m) / instances)
    return matrix


def near_scale(values):
    scales = 1.0 + np.arange(4096) / 4096.0
    scaled = scales[:, None] * values[None, :]
    rounded = scaled.astype(BF16).astype(np.float64)
    return float(scales[np.argmin(np.max(np.abs(rounded / scaled - 1.0), axis=1))])


def force_slots(passages, walls_k):
    pitch = up_to(walls_k * 8, 32)
    per_row = 128 // pitch
    return pitch, per_row, up_to(passages, per_row) // per_row * 128


def constants(layers, passages, walls_k):
    rows = HB * NV * layers
    padded = up_to(rows, 16)
    side = up_to(HB * NV, 16)
    width = padded + 2 * side
    harmonic = harmonic_matrix(HB)
    scale = near_scale(np.unique(np.abs(harmonic[harmonic != 0])))
    mix = np.zeros((padded, padded), np.float32)
    axial = np.zeros((padded, width), np.float32)
    fixed = np.zeros((3, padded, width), np.float32)
    pick = np.zeros((2 * side, padded), np.float32)
    weights = np.zeros((8, padded), np.int32)
    of_row = np.zeros((padded, NV), np.float32)
    of_column = np.zeros((NV, width), np.float32)
    for i in range(rows):
        r, a = divmod(i, layers)
        n, v = divmod(r, NV)
        of_row[i, v] = 1
        of_column[v, i] = 1
        of_column[v, padded + r] = 1
        of_column[v, padded + side + r] = 1
        weights[n, i] = v + 1
        if a == 0:
            pick[r, i] = 1
        if a == layers - 1:
            pick[side + r, i] = 1
        for w in range(NV):
            q = n * NV + w
            mix[i, q * layers + a] = 1
            axial[i, q * layers + a + 1 if a < layers - 1 else padded + q] = 1
            axial[i, q * layers + a - 1 if a > 0 else padded + side + q] = -1
        fixed[1, i, i] = -1
        fixed[1, i, i + 1 if a < layers - 1 else padded + r] = 1
        fixed[2, i, i] = -1
        fixed[2, i, i - 1 if a > 0 else padded + side + r] = 1
        for m in range(HB):
            fixed[0, i, (m * NV + v) * layers + a] = scale * harmonic[n, m]
    modes = np.zeros((up_to(walls_k * passages, 16), 2 * walls_k * passages), np.float32)
    for p in range(passages):
        for d in range(passages):
            angle = 2.0 * math.pi * (d * p % passages) / passages
            for k in range(walls_k):
                modes[p * walls_k + k, k * passages + d] = math.cos(angle)
                modes[p * walls_k + k, (walls_k + k) * passages + d] = -math.sin(angle)
    arrays = (
        mix.astype(BF16),
        axial.astype(BF16),
        fixed.reshape(3 * padded, width).astype(BF16),
        pick.astype(BF16),
        weights,
        of_row.astype(BF16),
        of_column.astype(BF16),
        modes,
    )
    return arrays, scale


def dot(a, b):
    return jnp.dot(a, b, preferred_element_type=F32)


def kernel(
    *refs, n_in, n_cell, n_circ, layers, padded, scale,
):
    sources = refs[:n_in]
    image, modal = refs[n_in : n_in + 2]
    held_in = refs[n_in + 2 : 2 * n_in + 2]
    (
        state, time_coef, axial_damp, plane_damp, periodic_damp, jac, faces, sides, face_map,
        wall_cells, normals, press_w, mode_shapes,
        mix_c, axial_c, fixed_c, pick_c, weights_c, of_row_c, of_column_c, modes_c,
    ) = held_in
    (
        extra, signed, joint, stack, cell_out, above, below, side_out, side_next, side_prev,
        forces, modes_high, modes_low, flux, total,
        cell_send, cell_recv, side_send, side_recv, force_send, force_recv, load_sem,
    ) = refs[2 * n_in + 2 :]
    me_cell = lax.axis_index("cell")
    me_circ = lax.axis_index("circ")
    me = me_circ * n_cell + me_cell

    def cell_at(j):
        return {"cell": lax.rem(me_cell + j, n_cell)}

    def circ_at(j):
        return {"circ": lax.rem(me_circ + j, n_circ)}

    def peer(i, j):
        return {"circ": lax.rem(me_circ + i, n_circ), "cell": lax.rem(me_cell + j, n_cell)}

    peers = [(i, j) for i in range(n_circ) for j in range(n_cell) if i or j]
    loads = {}

    def fetch(which):
        for at in which:
            loads[at] = pltpu.make_async_copy(sources[at], held_in[at], load_sem.at[at])
            loads[at].start()

    fetch(LOAD_ORDER[:2])
    peers = [(i, j) for i in range(n_circ) for j in range(n_cell) if i or j]
    barrier = pltpu.get_barrier_semaphore()
    for i, j in peers:
        pl.semaphore_signal(barrier, inc=1, device_id=peer(i, j), device_id_type=MESH)
    fetch(LOAD_ORDER[2:])

    def load(*which):
        for at in which:
            loads.pop(at).wait()

    n_rows, _, cells = state.shape
    n_faces = faces.shape[1]
    n_walls = wall_cells.shape[1]
    per = sides.shape[1]
    side_rows = above.shape[0]
    walls_k = normals.shape[0]
    groups = padded // 8

    def by_layer(value, pattern):
        return (value.reshape(groups, 8, value.shape[1]) * pattern[None]).reshape(value.shape)

    def pattern_of(rows):
        return jnp.concatenate([rows] * (8 // layers), axis=0)

    copies = []

    def send(source, target, send_sem, recv_sem, device):
        copy = pltpu.make_async_remote_copy(
            src_ref=source, dst_ref=target, send_sem=send_sem, recv_sem=recv_sem,
            device_id=device, device_id_type=MESH,
        )
        copy.start()
        copies.append(copy)
        return copy

    band = lax.broadcasted_iota(jnp.int32, (GROUP, 128), 0).astype(F32).astype(BF16)
    one = jnp.ones((GROUP, 128), BF16)
    zero = jnp.zeros((GROUP, 128), BF16)

    def spread(row):
        return jnp.broadcast_to(row.astype(F32).astype(BF16), (GROUP, 128))

    def split(row):
        high = lax.shift_right_logical(row, GROUP.bit_length() - 1)
        return spread(high), jnp.where(band == spread(row - high * GROUP), one, zero)

    def mark(columns, first):
        for at in range(0, columns.shape[1], 128):
            high, low = split(columns[:, at : at + 128])
            for h in range(cells // GROUP):
                hit = jnp.where(high == h, low, zero)
                here = slice(first + at, first + at + 128)
                extra[h * GROUP : (h + 1) * GROUP, here] = hit.astype(F8)

    load(WALL_CELLS)
    wall_index = wall_cells[...]
    wall_layer = lax.div(wall_index, cells)
    mark(wall_index - wall_layer * cells, 0)

    load(STATE)
    wide = state[...].astype(F32)
    pieces = [wide[r] for r in range(n_rows)]
    pieces.append(jnp.zeros((padded - n_rows * layers, cells), F32))
    u = jnp.concatenate(pieces, axis=0).astype(BF16)
    stack[0:padded, :] = u

    load(NORMALS, PRESS_W, WEIGHTS_C)
    gathered = dot(u, extra[:, 0:n_walls])
    layer_of = lax.rem(lax.broadcasted_iota(jnp.int32, (8, n_walls), 0), layers)
    here = by_layer(gathered, (layer_of == wall_layer).astype(F32)).astype(BF16)
    weight_class = weights_c[...]
    weight = jnp.zeros(weight_class.shape, F32)
    for v in range(NV):
        weight = jnp.where(weight_class == v + 1, press_w[v], weight)
    high = weight.astype(BF16)
    low = (weight - high.astype(F32)).astype(BF16)
    pressure = dot(high, here) + dot(low, here)
    pitch, per_row, _ = force_slots(n_circ, walls_k)
    lane = lax.broadcasted_iota(jnp.int32, (8, 128), 1)
    lane = lane - lax.broadcasted_iota(jnp.int32, (8, 128), 0) - lax.rem(me_circ, per_row) * pitch
    tile = jnp.zeros((8, 128), F32)
    for k in range(walls_k):
        force = jnp.sum(pressure * normals[k : k + 1, :], axis=1, keepdims=True)
        tile = jnp.where(lane == k * 8, force, tile)
    forces[me] = jnp.sum(tile, axis=0, keepdims=True)

    pl.semaphore_wait(barrier, n_cell * n_circ - 1)
    for i, j in peers:
        send(forces.at[me], forces.at[me], force_send, force_recv, peer(i, j))
    copies.clear()

    load(FACE_MAP, SIDES, PERIODIC_DAMP, AXIAL_DAMP, PICK_C)
    order = face_map[...]
    hits = (lax.broadcasted_iota(jnp.int32, (per, per), 0) == order).astype(F32)
    targets = jnp.dot(sides[0:1, :].astype(F32), hits, precision=HI, preferred_element_type=F32)
    targets = (targets + 0.5).astype(jnp.int32)
    mark(jnp.concatenate([sides[1:2, :], targets], axis=1), n_walls)

    cell_out[0 : 2 * side_rows, :] = dot(pick_c[...], u).astype(BF16)
    damp = axial_damp[0].astype(F32)
    last = damp[layers - 1 : layers]
    cell_out[2 * side_rows :, :] = jnp.broadcast_to(last, (16, cells)).astype(BF16)
    to_below = send(
        cell_out.at[pl.ds(0, side_rows)], above, cell_send.at[0], cell_recv.at[0],
        cell_at(n_cell - 1),
    )
    to_above = send(
        cell_out.at[pl.ds(side_rows, side_rows + 16)], below, cell_send.at[1], cell_recv.at[1],
        cell_at(1),
    )

    own_side = dot(u, extra[:, n_walls:])
    side_out[0:padded, :] = own_side.astype(BF16)
    side_damp = periodic_damp[0].astype(F32)
    side_pattern = pattern_of(jnp.concatenate([side_damp, side_damp], axis=1))
    side_out[padded:, :] = jnp.concatenate([side_pattern, side_pattern], axis=0).astype(BF16)
    to_prev = send(side_out, side_next, side_send.at[0], side_recv.at[0], circ_at(n_circ - 1))
    to_next = send(side_out, side_prev, side_send.at[1], side_recv.at[1], circ_at(1))

    load(JAC, OF_ROW_C, OF_COLUMN_C, MIX_C, AXIAL_C, PLANE_DAMP, FACES)

    def mixing(face, mask):
        values = (0.5 * jac[:, face, :]).astype(BF16)
        across = dot(values, of_column_c[:, : mask.shape[1]]).astype(BF16)
        return (dot(of_row_c[...], across) * mask.astype(F32)).astype(BF16)

    axial_mix = mixing(0, axial_c[...])
    plane_mix = mixing(1, mix_c[...])
    side_mix = mixing(2, mix_c[...])

    convected = dot(plane_mix, u).astype(BF16)
    plane_pattern = pattern_of(0.5 * plane_damp[0].astype(F32))

    def build(first, count):
        for at in range(first, first + count, 128):
            owner_high, owner = split(faces[0:1, at : at + 128])
            other_high, other = split(faces[1:2, at : at + 128])
            same = owner_high == other_high
            both = owner - other
            by_owner = jnp.where(same, both, owner)
            by_other = jnp.where(same, both, -other)
            for h in range(cells // GROUP):
                hit = jnp.where(other_high == h, by_other, zero)
                hit = jnp.where(owner_high == h, by_owner, hit)
                here = slice(h * GROUP, (h + 1) * GROUP)
                signed[here, at : at + 128] = hit.astype(F8)
                joint[here, at : at + 128] = jnp.abs(hit).astype(F8)

    def gather(first, count):
        here = slice(first, first + count)
        damped = by_layer(dot(u, signed[:, here]), plane_pattern[:, here])
        flux[:, here] = (dot(convected, joint[:, here]) + damped).astype(BF16)

    part = 256
    starts = list(range(0, n_faces, part))
    build(0, part)
    for at in starts:
        if at + part < n_faces:
            build(at + part, part)
        gather(at, part)

    load(MODE_SHAPES, MODES_C)
    shapes = mode_shapes[...].reshape(2 * walls_k * n_circ, mode_shapes.shape[3])
    by_passage = jnp.dot(modes_c[...], shapes, precision=HI, preferred_element_type=F32)
    modes_high[...] = jnp.zeros(modes_high.shape, BF16)
    modes_low[...] = jnp.zeros(modes_low.shape, BF16)
    for p in range(n_circ):
        first = p // per_row * 128 + p % per_row * pitch
        rows = [by_passage[p * walls_k + k : p * walls_k + k + 1] for k in range(walls_k)]
        rows = [jnp.broadcast_to(row, (8, row.shape[1])) for row in rows]
        rows += [jnp.zeros_like(rows[0])] * (pitch // 8 - walls_k)
        rows = jnp.concatenate(rows, axis=0)
        high = rows.astype(BF16)
        modes_high[first : first + pitch, :] = high
        modes_low[first : first + pitch, :] = (rows - high.astype(F32)).astype(BF16)

    total[...] = lax.dot_general(
        flux[...], signed[...], NT, preferred_element_type=F32
    )

    to_below.wait_recv()
    to_above.wait_recv()
    load(FIXED_C, TIME_COEF)
    above_rows = above[...].astype(F32)
    stack[padded : padded + side_rows, :] = jnp.where(
        me_cell == n_cell - 1, 0.0, above_rows
    ).astype(BF16)
    below_rows = below[0:side_rows, :].astype(F32)
    stack[padded + side_rows :, :] = jnp.where(
        me_cell == 0, -cell_out[0:side_rows, :].astype(F32), below_rows
    ).astype(BF16)
    below_damp = below[side_rows : side_rows + 16, :].astype(F32)[0:1]
    below_damp = jnp.where(me_cell == 0, 0.0, below_damp)
    held = stack[...]
    derived = dot(fixed_c[...], held)
    result = by_layer(derived[0:padded], pattern_of(time_coef[0] * (1.0 / scale)))
    result = result - by_layer(derived[padded : 2 * padded], pattern_of(0.5 * damp))
    lower_damp = jnp.concatenate([below_damp, damp[0 : layers - 1]], axis=0)
    result = result - by_layer(derived[2 * padded :], pattern_of(0.5 * lower_damp))
    result = result + dot(axial_mix, held)

    to_prev.wait_recv()
    to_next.wait_recv()
    left = lax.broadcasted_iota(jnp.int32, (padded, 2 * per), 1) < per
    ahead = pltpu.roll(side_next[0:padded, :].astype(F32), per, 1)
    back = pltpu.roll(side_prev[0:padded, :].astype(F32), per, 1)
    back_damp = side_prev[padded:, :].astype(F32)[0:8]
    lower = jnp.where(left, own_side, back)
    upper = jnp.where(left, ahead, own_side)
    side_s = 0.5 * jnp.where(left[0:8], side_pattern, back_damp)
    lower_b, upper_b = lower.astype(BF16), upper.astype(BF16)
    side_flux = dot(side_mix, lower_b) + dot(side_mix, upper_b)
    side_flux = side_flux - by_layer(upper - lower, side_s)
    side_flux = jnp.where(left, side_flux, -side_flux).astype(BF16)
    result = result + lax.dot_general(
        side_flux, extra[:, n_walls:], NT, preferred_element_type=F32
    )
    result = result + total[...]
    for r in range(n_rows):
        image[r] = result[r * layers : (r + 1) * layers].astype(BF16)

    others = n_cell * n_circ - 1
    arrived = pltpu.make_async_remote_copy(
        src_ref=forces.at[pl.ds(0, others)], dst_ref=forces.at[pl.ds(0, others)],
        send_sem=force_send, recv_sem=force_recv, device_id=peer(0, 1), device_id_type=MESH,
    )
    arrived.wait_recv()
    sublane = lax.broadcasted_iota(jnp.int32, (8, 128), 0)
    kept = lax.rem(lax.broadcasted_iota(jnp.int32, (8, 128), 1), 8) == sublane
    rows = []
    for first in range(0, n_circ, per_row):
        slots = range(first * n_cell, min(first + per_row, n_circ) * n_cell)
        row = [forces[slot] for slot in slots]
        while len(row) > 1:
            row = [a + b for a, b in zip(row[::2], row[1::2])] + row[len(row) // 2 * 2 :]
        rows.append(jnp.where(kept, jnp.broadcast_to(row[0], (8, 128)), 0.0))
    every = jnp.concatenate(rows, axis=1)
    high = every.astype(BF16)
    low = (every - high.astype(F32)).astype(BF16)
    table = modes_high[...]
    answer = dot(high, table) + dot(low, table) + dot(high, modes_low[...])
    modal[...] = answer[0:HB]
    arrived.wait_send()
    for copy in copies:
        copy.wait_send()


def deliver(image, modal, image_out, modal_out, sems):
    copies = [
        pltpu.make_async_copy(image, image_out, sems.at[0]),
        pltpu.make_async_copy(modal, modal_out, sems.at[1]),
    ]
    for copy in copies:
        copy.start()
    for copy in copies:
        copy.wait()


def shards(
    flow_state, time_coef, axial_damp, plane_damp, periodic_damp, flux_jacobian, face_cells,
    periodic_cells, face_map, wall_cells, wall_normals, pressure_weights, mode_shapes,
):
    layers, cells = flow_state.shape[2:]
    n_cell = lax.axis_size("cell")
    n_circ = lax.axis_size("circ")
    walls_k = wall_normals.shape[0]
    n_modes = mode_shapes.shape[3]
    per = face_map.shape[0]
    n_faces = face_cells.shape[1]
    n_walls = wall_cells.shape[0]
    fixed, scale = constants(layers, n_circ, walls_k)
    padded = fixed[0].shape[0]
    side = fixed[3].shape[0] // 2
    lanes = force_slots(n_circ, walls_k)[2]
    state = flow_state.reshape(HB * NV, layers, cells)
    vmem = pl.BlockSpec(memory_space=pltpu.VMEM)
    dma = pltpu.SemaphoreType.DMA
    operands = (
        state, time_coef, axial_damp, plane_damp, periodic_damp,
        flux_jacobian.transpose(1, 0, 2), face_cells, periodic_cells, face_map[None],
        wall_cells[None], wall_normals, pressure_weights,
        mode_shapes.transpose(0, 2, 1, 3), *(jnp.asarray(array) for array in fixed),
    )
    hbm = pl.BlockSpec(memory_space=pltpu.HBM)
    held = [
        (pltpu.SMEM if at == PRESS_W else pltpu.VMEM)(array.shape, array.dtype)
        for at, array in enumerate(operands)
    ]
    image, modal = pl.pallas_call(
        functools.partial(
            kernel, n_in=len(operands), n_cell=n_cell, n_circ=n_circ, layers=layers,
            padded=padded, scale=scale,
        ),
        out_shape=(
            jax.ShapeDtypeStruct((HB * NV, layers, cells), BF16),
            jax.ShapeDtypeStruct((HB, n_modes), F32),
        ),
        in_specs=[hbm] * len(operands),
        out_specs=(vmem, vmem),
        scratch_shapes=[
            *held,
            pltpu.VMEM((cells, n_walls + 2 * per), F8),
            pltpu.VMEM((cells, n_faces), F8),
            pltpu.VMEM((cells, n_faces), F8),
            pltpu.VMEM((padded + 2 * side, cells), BF16),
            pltpu.VMEM((2 * side + 16, cells), BF16),
            pltpu.VMEM((side, cells), BF16),
            pltpu.VMEM((side + 16, cells), BF16),
            pltpu.VMEM((padded + 16, 2 * per), BF16),
            pltpu.VMEM((padded + 16, 2 * per), BF16),
            pltpu.VMEM((padded + 16, 2 * per), BF16),
            pltpu.VMEM((n_circ * n_cell, 1, 128), F32),
            pltpu.VMEM((lanes, n_modes), BF16),
            pltpu.VMEM((lanes, n_modes), BF16),
            pltpu.VMEM((padded, n_faces), BF16),
            pltpu.VMEM((padded, cells), F32),
            dma((2,)), dma((2,)), dma((2,)), dma((2,)), dma, dma, dma((len(operands),)),
        ],
        compiler_params=pltpu.CompilerParams(
            collective_id=0, has_side_effects=True, vmem_limit_bytes=VMEM_LIMIT
        ),
    )(*(pltpu.with_memory_space_constraint(array, pltpu.HBM) for array in operands))
    image, modal = pl.pallas_call(
        deliver,
        out_shape=(
            jax.ShapeDtypeStruct(image.shape, BF16),
            jax.ShapeDtypeStruct(modal.shape, F32),
        ),
        in_specs=[vmem] * 2,
        out_specs=(hbm, hbm),
        scratch_shapes=[dma((2,))],
        compiler_params=pltpu.CompilerParams(vmem_limit_bytes=VMEM_LIMIT),
    )(image, modal)
    return image.reshape(HB * NV, 1, layers, cells), modal


def solution(mesh):
    circ = P("circ", "cell", None)
    placed = (
        P(None, "circ", "cell", None), circ, circ, circ, circ, P(), P(), P(), P(),
        P("cell"), P(None, "cell"), P(), P(),
    )
    return jax.shard_map(
        shards,
        mesh=mesh,
        in_specs=placed,
        out_specs=(P(None, "circ", "cell", None), P()),
        check_vma=False,
    )
```

```python
import functools
import math

import jax
import jax.numpy as jnp
import numpy as np
from jax import lax
from jax.experimental import pallas as pl
from jax.experimental.pallas import tpu as pltpu
from jax.sharding import PartitionSpec as P

NV = 5
HB = 7
F32 = jnp.float32
BF16 = jnp.bfloat16
F8 = jnp.float8_e4m3fn
GROUP = 32
VMEM_LIMIT = 24 << 20
(
    STATE, TIME_COEF, AXIAL_DAMP, PLANE_DAMP, PERIODIC_DAMP, JAC, FACES, SIDES, FACE_MAP,
    WALL_CELLS, NORMALS, PRESS_W, MODE_SHAPES,
    MIX_C, AXIAL_C, FIXED_C, PICK_C, WEIGHTS_C, OF_ROW_C, OF_COLUMN_C, MODES_C,
) = range(21)
LOAD_ORDER = (
    STATE, WALL_CELLS, NORMALS, PRESS_W, WEIGHTS_C, FACE_MAP, SIDES, PERIODIC_DAMP, AXIAL_DAMP,
    PICK_C, JAC, OF_ROW_C, OF_COLUMN_C, MIX_C, AXIAL_C, PLANE_DAMP, FACES, MODE_SHAPES, MODES_C,
    FIXED_C, TIME_COEF,
)
HI = lax.Precision.HIGHEST
MESH = pl.DeviceIdType.MESH
NT = (((1,), (1,)), ((), ()))


def up_to(value, step):
    return -(-value // step) * step


def harmonic_matrix(instances):
    matrix = np.zeros((instances, instances))
    for n in range(instances):
        for m in range(instances):
            if n != m:
                matrix[n, m] = 0.5 * (-1.0) ** (n - m) / math.sin(math.pi * (n - m) / instances)
    return matrix


def near_scale(values):
    scales = 1.0 + np.arange(4096) / 4096.0
    scaled = scales[:, None] * values[None, :]
    rounded = scaled.astype(BF16).astype(np.float64)
    return float(scales[np.argmin(np.max(np.abs(rounded / scaled - 1.0), axis=1))])


def force_slots(passages, walls_k):
    pitch = up_to(walls_k * 8, 32)
    per_row = 128 // pitch
    return pitch, per_row, up_to(passages, per_row) // per_row * 128


def constants(layers, passages, walls_k):
    rows = HB * NV * layers
    padded = up_to(rows, 16)
    side = up_to(HB * NV, 16)
    width = padded + 2 * side
    harmonic = harmonic_matrix(HB)
    scale = near_scale(np.unique(np.abs(harmonic[harmonic != 0])))
    mix = np.zeros((padded, padded), np.float32)
    axial = np.zeros((padded, width), np.float32)
    fixed = np.zeros((3, padded, width), np.float32)
    pick = np.zeros((2 * side, padded), np.float32)
    weights = np.zeros((8, padded), np.int32)
    of_row = np.zeros((padded, NV), np.float32)
    of_column = np.zeros((NV, width), np.float32)
    for i in range(rows):
        r, a = divmod(i, layers)
        n, v = divmod(r, NV)
        of_row[i, v] = 1
        of_column[v, i] = 1
        of_column[v, padded + r] = 1
        of_column[v, padded + side + r] = 1
        weights[n, i] = v + 1
        if a == 0:
            pick[r, i] = 1
        if a == layers - 1:
            pick[side + r, i] = 1
        for w in range(NV):
            q = n * NV + w
            mix[i, q * layers + a] = 1
            axial[i, q * layers + a + 1 if a < layers - 1 else padded + q] = 1
            axial[i, q * layers + a - 1 if a > 0 else padded + side + q] = -1
        fixed[1, i, i] = -1
        fixed[1, i, i + 1 if a < layers - 1 else padded + r] = 1
        fixed[2, i, i] = -1
        fixed[2, i, i - 1 if a > 0 else padded + side + r] = 1
        for m in range(HB):
            fixed[0, i, (m * NV + v) * layers + a] = scale * harmonic[n, m]
    modes = np.zeros((up_to(walls_k * passages, 16), 2 * walls_k * passages), np.float32)
    for p in range(passages):
        for d in range(passages):
            angle = 2.0 * math.pi * (d * p % passages) / passages
            for k in range(walls_k):
                modes[p * walls_k + k, k * passages + d] = math.cos(angle)
                modes[p * walls_k + k, (walls_k + k) * passages + d] = -math.sin(angle)
    arrays = (
        mix.astype(BF16),
        axial.astype(BF16),
        fixed.reshape(3 * padded, width).astype(BF16),
        pick.astype(BF16),
        weights,
        of_row.astype(BF16),
        of_column.astype(BF16),
        modes,
    )
    return arrays, scale


def dot(a, b):
    return jnp.dot(a, b, preferred_element_type=F32)


def kernel(
    *refs, n_in, n_cell, n_circ, layers, padded, scale,
):
    sources = refs[:n_in]
    image, modal = refs[n_in : n_in + 2]
    held_in = refs[n_in + 2 : 2 * n_in + 2]
    (
        state, time_coef, axial_damp, plane_damp, periodic_damp, jac, faces, sides, face_map,
        wall_cells, normals, press_w, mode_shapes,
        mix_c, axial_c, fixed_c, pick_c, weights_c, of_row_c, of_column_c, modes_c,
    ) = held_in
    (
        extra, signed, joint, stack, cell_out, above, below, side_out, side_next, side_prev,
        forces, modes_high, modes_low, flux, total,
        cell_send, cell_recv, side_send, side_recv, force_send, force_recv, load_sem,
    ) = refs[2 * n_in + 2 :]
    me_cell = lax.axis_index("cell")
    me_circ = lax.axis_index("circ")
    me = me_circ * n_cell + me_cell

    def cell_at(j):
        return {"cell": lax.rem(me_cell + j, n_cell)}

    def circ_at(j):
        return {"circ": lax.rem(me_circ + j, n_circ)}

    def peer(i, j):
        return {"circ": lax.rem(me_circ + i, n_circ), "cell": lax.rem(me_cell + j, n_cell)}

    peers = [(i, j) for i in range(n_circ) for j in range(n_cell) if i or j]
    loads = {}

    def fetch(which):
        for at in which:
            loads[at] = pltpu.make_async_copy(sources[at], held_in[at], load_sem.at[at])
            loads[at].start()

    fetch(LOAD_ORDER[:2])
    peers = [(i, j) for i in range(n_circ) for j in range(n_cell) if i or j]
    barrier = pltpu.get_barrier_semaphore()
    for i, j in peers:
        pl.semaphore_signal(barrier, inc=1, device_id=peer(i, j), device_id_type=MESH)
    fetch(LOAD_ORDER[2:])

    def load(*which):
        for at in which:
            loads.pop(at).wait()

    n_rows, _, cells = state.shape
    n_faces = faces.shape[1]
    n_walls = wall_cells.shape[1]
    per = sides.shape[1]
    side_rows = above.shape[0]
    walls_k = normals.shape[0]
    groups = padded // 8

    def by_layer(value, pattern):
        return (value.reshape(groups, 8, value.shape[1]) * pattern[None]).reshape(value.shape)

    def pattern_of(rows):
        return jnp.concatenate([rows] * (8 // layers), axis=0)

    def remote(source, target, send_sem, recv_sem, device):
        return pltpu.make_async_remote_copy(
            src_ref=source, dst_ref=target, send_sem=send_sem, recv_sem=recv_sem,
            device_id=device, device_id_type=MESH,
        )

    to_below = remote(
        cell_out.at[pl.ds(0, side_rows)], above, cell_send.at[0], cell_recv.at[0],
        cell_at(n_cell - 1),
    )
    to_above = remote(
        cell_out.at[pl.ds(side_rows, side_rows + 16)], below, cell_send.at[1], cell_recv.at[1],
        cell_at(1),
    )
    to_prev = remote(side_out, side_next, side_send.at[0], side_recv.at[0], circ_at(n_circ - 1))
    to_next = remote(side_out, side_prev, side_send.at[1], side_recv.at[1], circ_at(1))
    copies = [to_below, to_above, to_prev, to_next]

    def send_sides():
        for copy in copies:
            copy.start()

    band = lax.broadcasted_iota(jnp.int32, (GROUP, 128), 0).astype(F32).astype(BF16)
    one = jnp.ones((GROUP, 128), BF16)
    zero = jnp.zeros((GROUP, 128), BF16)

    def spread(row):
        return jnp.broadcast_to(row.astype(F32).astype(BF16), (GROUP, 128))

    def split(row):
        high = lax.shift_right_logical(row, GROUP.bit_length() - 1)
        return spread(high), jnp.where(band == spread(row - high * GROUP), one, zero)

    def mark(columns, first):
        for at in range(0, columns.shape[1], 128):
            high, low = split(columns[:, at : at + 128])
            for h in range(cells // GROUP):
                hit = jnp.where(high == h, low, zero)
                here = slice(first + at, first + at + 128)
                extra[h * GROUP : (h + 1) * GROUP, here] = hit.astype(F8)

    load(WALL_CELLS)
    wall_index = wall_cells[...]
    wall_layer = lax.div(wall_index, cells)
    mark(wall_index - wall_layer * cells, 0)

    load(STATE)
    wide = state[...].astype(F32)
    pieces = [wide[r] for r in range(n_rows)]
    pieces.append(jnp.zeros((padded - n_rows * layers, cells), F32))
    u = jnp.concatenate(pieces, axis=0).astype(BF16)
    stack[0:padded, :] = u

    load(NORMALS, PRESS_W, WEIGHTS_C)
    gathered = dot(u, extra[:, 0:n_walls])
    layer_of = lax.rem(lax.broadcasted_iota(jnp.int32, (8, n_walls), 0), layers)
    here = by_layer(gathered, (layer_of == wall_layer).astype(F32)).astype(BF16)
    weight_class = weights_c[...]
    weight = jnp.zeros(weight_class.shape, F32)
    for v in range(NV):
        weight = jnp.where(weight_class == v + 1, press_w[v], weight)
    high = weight.astype(BF16)
    low = (weight - high.astype(F32)).astype(BF16)
    pressure = dot(high, here) + dot(low, here)
    pitch, per_row, _ = force_slots(n_circ, walls_k)
    lane = lax.broadcasted_iota(jnp.int32, (8, 128), 1)
    lane = lane - lax.broadcasted_iota(jnp.int32, (8, 128), 0) - lax.rem(me_circ, per_row) * pitch
    tile = jnp.zeros((8, 128), F32)
    for k in range(walls_k):
        force = jnp.sum(pressure * normals[k : k + 1, :], axis=1, keepdims=True)
        tile = jnp.where(lane == k * 8, force, tile)
    forces[me] = jnp.sum(tile, axis=0, keepdims=True)

    late = me_circ >= n_circ // 2

    def enter_and_send_forces():
        pl.semaphore_wait(barrier, n_cell * n_circ - 1)
        for i, j in peers:
            remote(forces.at[me], forces.at[me], force_send, force_recv, peer(i, j)).start()

    pl.when(late)(enter_and_send_forces)

    load(FACE_MAP, SIDES, PERIODIC_DAMP, AXIAL_DAMP, PICK_C)
    order = face_map[...]
    hits = (lax.broadcasted_iota(jnp.int32, (per, per), 0) == order).astype(F32)
    targets = jnp.dot(sides[0:1, :].astype(F32), hits, precision=HI, preferred_element_type=F32)
    targets = (targets + 0.5).astype(jnp.int32)
    mark(jnp.concatenate([sides[1:2, :], targets], axis=1), n_walls)

    cell_out[0 : 2 * side_rows, :] = dot(pick_c[...], u).astype(BF16)
    damp = axial_damp[0].astype(F32)
    last = damp[layers - 1 : layers]
    cell_out[2 * side_rows :, :] = jnp.broadcast_to(last, (16, cells)).astype(BF16)
    own_side = dot(u, extra[:, n_walls:])
    side_out[0:padded, :] = own_side.astype(BF16)
    side_damp = periodic_damp[0].astype(F32)
    side_pattern = pattern_of(jnp.concatenate([side_damp, side_damp], axis=1))
    side_out[padded:, :] = jnp.concatenate([side_pattern, side_pattern], axis=0).astype(BF16)
    pl.when(late)(send_sides)

    load(JAC, OF_ROW_C, OF_COLUMN_C, MIX_C, AXIAL_C, PLANE_DAMP, FACES)

    def mixing(face, mask):
        values = (0.5 * jac[:, face, :]).astype(BF16)
        across = dot(values, of_column_c[:, : mask.shape[1]]).astype(BF16)
        return (dot(of_row_c[...], across) * mask.astype(F32)).astype(BF16)

    axial_mix = mixing(0, axial_c[...])
    plane_mix = mixing(1, mix_c[...])
    side_mix = mixing(2, mix_c[...])

    convected = dot(plane_mix, u).astype(BF16)
    plane_pattern = pattern_of(0.5 * plane_damp[0].astype(F32))

    def build(first, count):
        for at in range(first, first + count, 128):
            owner_high, owner = split(faces[0:1, at : at + 128])
            other_high, other = split(faces[1:2, at : at + 128])
            same = owner_high == other_high
            both = owner - other
            by_owner = jnp.where(same, both, owner)
            by_other = jnp.where(same, both, -other)
            for h in range(cells // GROUP):
                hit = jnp.where(other_high == h, by_other, zero)
                hit = jnp.where(owner_high == h, by_owner, hit)
                here = slice(h * GROUP, (h + 1) * GROUP)
                signed[here, at : at + 128] = hit.astype(F8)
                joint[here, at : at + 128] = jnp.abs(hit).astype(F8)

    def gather(first, count):
        here = slice(first, first + count)
        damped = by_layer(dot(u, signed[:, here]), plane_pattern[:, here])
        flux[:, here] = (dot(convected, joint[:, here]) + damped).astype(BF16)

    part = 256
    starts = list(range(0, n_faces, part))
    build(0, part)
    for at in starts:
        if at + part < n_faces:
            build(at + part, part)
        gather(at, part)

    load(MODE_SHAPES, MODES_C)
    shapes = mode_shapes[...].reshape(2 * walls_k * n_circ, mode_shapes.shape[3])
    by_passage = jnp.dot(modes_c[...], shapes, precision=HI, preferred_element_type=F32)
    modes_high[...] = jnp.zeros(modes_high.shape, BF16)
    modes_low[...] = jnp.zeros(modes_low.shape, BF16)
    for p in range(n_circ):
        first = p // per_row * 128 + p % per_row * pitch
        rows = [by_passage[p * walls_k + k : p * walls_k + k + 1] for k in range(walls_k)]
        rows = [jnp.broadcast_to(row, (8, row.shape[1])) for row in rows]
        rows += [jnp.zeros_like(rows[0])] * (pitch // 8 - walls_k)
        rows = jnp.concatenate(rows, axis=0)
        high = rows.astype(BF16)
        modes_high[first : first + pitch, :] = high
        modes_low[first : first + pitch, :] = (rows - high.astype(F32)).astype(BF16)

    total[...] = lax.dot_general(
        flux[...], signed[...], NT, preferred_element_type=F32
    )

    @pl.when(jnp.logical_not(late))
    def _():
        enter_and_send_forces()
        send_sides()

    to_below.wait_recv()
    to_above.wait_recv()
    load(FIXED_C, TIME_COEF)
    above_rows = above[...].astype(F32)
    stack[padded : padded + side_rows, :] = jnp.where(
        me_cell == n_cell - 1, 0.0, above_rows
    ).astype(BF16)
    below_rows = below[0:side_rows, :].astype(F32)
    stack[padded + side_rows :, :] = jnp.where(
        me_cell == 0, -cell_out[0:side_rows, :].astype(F32), below_rows
    ).astype(BF16)
    below_damp = below[side_rows : side_rows + 16, :].astype(F32)[0:1]
    below_damp = jnp.where(me_cell == 0, 0.0, below_damp)
    held = stack[...]
    derived = dot(fixed_c[...], held)
    result = by_layer(derived[0:padded], pattern_of(time_coef[0] * (1.0 / scale)))
    result = result - by_layer(derived[padded : 2 * padded], pattern_of(0.5 * damp))
    lower_damp = jnp.concatenate([below_damp, damp[0 : layers - 1]], axis=0)
    result = result - by_layer(derived[2 * padded :], pattern_of(0.5 * lower_damp))
    result = result + dot(axial_mix, held)

    to_prev.wait_recv()
    to_next.wait_recv()
    left = lax.broadcasted_iota(jnp.int32, (padded, 2 * per), 1) < per
    ahead = pltpu.roll(side_next[0:padded, :].astype(F32), per, 1)
    back = pltpu.roll(side_prev[0:padded, :].astype(F32), per, 1)
    back_damp = side_prev[padded:, :].astype(F32)[0:8]
    lower = jnp.where(left, own_side, back)
    upper = jnp.where(left, ahead, own_side)
    side_s = 0.5 * jnp.where(left[0:8], side_pattern, back_damp)
    lower_b, upper_b = lower.astype(BF16), upper.astype(BF16)
    side_flux = dot(side_mix, lower_b) + dot(side_mix, upper_b)
    side_flux = side_flux - by_layer(upper - lower, side_s)
    side_flux = jnp.where(left, side_flux, -side_flux).astype(BF16)
    result = result + lax.dot_general(
        side_flux, extra[:, n_walls:], NT, preferred_element_type=F32
    )
    result = result + total[...]
    for r in range(n_rows):
        image[r] = result[r * layers : (r + 1) * layers].astype(BF16)

    others = n_cell * n_circ - 1
    arrived = pltpu.make_async_remote_copy(
        src_ref=forces.at[pl.ds(0, others)], dst_ref=forces.at[pl.ds(0, others)],
        send_sem=force_send, recv_sem=force_recv, device_id=peer(0, 1), device_id_type=MESH,
    )
    arrived.wait_recv()
    sublane = lax.broadcasted_iota(jnp.int32, (8, 128), 0)
    kept = lax.rem(lax.broadcasted_iota(jnp.int32, (8, 128), 1), 8) == sublane
    rows = []
    for first in range(0, n_circ, per_row):
        slots = range(first * n_cell, min(first + per_row, n_circ) * n_cell)
        row = [forces[slot] for slot in slots]
        while len(row) > 1:
            row = [a + b for a, b in zip(row[::2], row[1::2])] + row[len(row) // 2 * 2 :]
        rows.append(jnp.where(kept, jnp.broadcast_to(row[0], (8, 128)), 0.0))
    every = jnp.concatenate(rows, axis=1)
    high = every.astype(BF16)
    low = (every - high.astype(F32)).astype(BF16)
    table = modes_high[...]
    answer = dot(high, table) + dot(low, table) + dot(high, modes_low[...])
    modal[...] = answer[0:HB]
    arrived.wait_send()
    for copy in copies:
        copy.wait_send()


def deliver(image, modal, image_out, modal_out, sems):
    copies = [
        pltpu.make_async_copy(image, image_out, sems.at[0]),
        pltpu.make_async_copy(modal, modal_out, sems.at[1]),
    ]
    for copy in copies:
        copy.start()
    for copy in copies:
        copy.wait()


def shards(
    flow_state, time_coef, axial_damp, plane_damp, periodic_damp, flux_jacobian, face_cells,
    periodic_cells, face_map, wall_cells, wall_normals, pressure_weights, mode_shapes,
):
    layers, cells = flow_state.shape[2:]
    n_cell = lax.axis_size("cell")
    n_circ = lax.axis_size("circ")
    walls_k = wall_normals.shape[0]
    n_modes = mode_shapes.shape[3]
    per = face_map.shape[0]
    n_faces = face_cells.shape[1]
    n_walls = wall_cells.shape[0]
    fixed, scale = constants(layers, n_circ, walls_k)
    padded = fixed[0].shape[0]
    side = fixed[3].shape[0] // 2
    lanes = force_slots(n_circ, walls_k)[2]
    state = flow_state.reshape(HB * NV, layers, cells)
    vmem = pl.BlockSpec(memory_space=pltpu.VMEM)
    dma = pltpu.SemaphoreType.DMA
    operands = (
        state, time_coef, axial_damp, plane_damp, periodic_damp,
        flux_jacobian.transpose(1, 0, 2), face_cells, periodic_cells, face_map[None],
        wall_cells[None], wall_normals, pressure_weights,
        mode_shapes.transpose(0, 2, 1, 3), *(jnp.asarray(array) for array in fixed),
    )
    hbm = pl.BlockSpec(memory_space=pltpu.HBM)
    held = [
        (pltpu.SMEM if at == PRESS_W else pltpu.VMEM)(array.shape, array.dtype)
        for at, array in enumerate(operands)
    ]
    image, modal = pl.pallas_call(
        functools.partial(
            kernel, n_in=len(operands), n_cell=n_cell, n_circ=n_circ, layers=layers,
            padded=padded, scale=scale,
        ),
        out_shape=(
            jax.ShapeDtypeStruct((HB * NV, layers, cells), BF16),
            jax.ShapeDtypeStruct((HB, n_modes), F32),
        ),
        in_specs=[hbm] * len(operands),
        out_specs=(vmem, vmem),
        scratch_shapes=[
            *held,
            pltpu.VMEM((cells, n_walls + 2 * per), F8),
            pltpu.VMEM((cells, n_faces), F8),
            pltpu.VMEM((cells, n_faces), F8),
            pltpu.VMEM((padded + 2 * side, cells), BF16),
            pltpu.VMEM((2 * side + 16, cells), BF16),
            pltpu.VMEM((side, cells), BF16),
            pltpu.VMEM((side + 16, cells), BF16),
            pltpu.VMEM((padded + 16, 2 * per), BF16),
            pltpu.VMEM((padded + 16, 2 * per), BF16),
            pltpu.VMEM((padded + 16, 2 * per), BF16),
            pltpu.VMEM((n_circ * n_cell, 1, 128), F32),
            pltpu.VMEM((lanes, n_modes), BF16),
            pltpu.VMEM((lanes, n_modes), BF16),
            pltpu.VMEM((padded, n_faces), BF16),
            pltpu.VMEM((padded, cells), F32),
            dma((2,)), dma((2,)), dma((2,)), dma((2,)), dma, dma, dma((len(operands),)),
        ],
        compiler_params=pltpu.CompilerParams(
            collective_id=0, has_side_effects=True, vmem_limit_bytes=VMEM_LIMIT
        ),
    )(*(pltpu.with_memory_space_constraint(array, pltpu.HBM) for array in operands))
    image, modal = pl.pallas_call(
        deliver,
        out_shape=(
            jax.ShapeDtypeStruct(image.shape, BF16),
            jax.ShapeDtypeStruct(modal.shape, F32),
        ),
        in_specs=[vmem] * 2,
        out_specs=(hbm, hbm),
        scratch_shapes=[dma((2,))],
        compiler_params=pltpu.CompilerParams(vmem_limit_bytes=VMEM_LIMIT),
    )(image, modal)
    return image.reshape(HB * NV, 1, layers, cells), modal


def solution(mesh):
    circ = P("circ", "cell", None)
    placed = (
        P(None, "circ", "cell", None), circ, circ, circ, circ, P(), P(), P(), P(),
        P("cell"), P(None, "cell"), P(), P(),
    )
    return jax.shard_map(
        shards,
        mesh=mesh,
        in_specs=placed,
        out_specs=(P(None, "circ", "cell", None), P()),
        check_vma=False,
    )
```

```python
import functools
import math

import jax
import jax.numpy as jnp
import numpy as np
from jax import lax
from jax.experimental import pallas as pl
from jax.experimental.pallas import tpu as pltpu
from jax.sharding import PartitionSpec as P

NV = 5
HB = 7
F32 = jnp.float32
BF16 = jnp.bfloat16
F8 = jnp.float8_e4m3fn
GROUP = 32
VMEM_LIMIT = 24 << 20
(
    STATE, TIME_COEF, AXIAL_DAMP, PLANE_DAMP, PERIODIC_DAMP, JAC, FACES, SIDES, FACE_MAP,
    WALL_CELLS, NORMALS, PRESS_W, MODE_SHAPES,
    MIX_C, AXIAL_C, FIXED_C, PICK_C, WEIGHTS_C, OF_ROW_C, OF_COLUMN_C, MODES_C,
) = range(21)
LOAD_ORDER = (
    STATE, WALL_CELLS, NORMALS, PRESS_W, WEIGHTS_C, FACE_MAP, SIDES, PERIODIC_DAMP, AXIAL_DAMP,
    PICK_C, JAC, OF_ROW_C, OF_COLUMN_C, MIX_C, AXIAL_C, PLANE_DAMP, FACES, MODE_SHAPES, MODES_C,
    FIXED_C, TIME_COEF,
)
HI = lax.Precision.HIGHEST
MESH = pl.DeviceIdType.MESH
NT = (((1,), (1,)), ((), ()))


def up_to(value, step):
    return -(-value // step) * step


def harmonic_matrix(instances):
    matrix = np.zeros((instances, instances))
    for n in range(instances):
        for m in range(instances):
            if n != m:
                matrix[n, m] = 0.5 * (-1.0) ** (n - m) / math.sin(math.pi * (n - m) / instances)
    return matrix


def near_scale(values):
    scales = 1.0 + np.arange(4096) / 4096.0
    scaled = scales[:, None] * values[None, :]
    rounded = scaled.astype(BF16).astype(np.float64)
    return float(scales[np.argmin(np.max(np.abs(rounded / scaled - 1.0), axis=1))])


def force_slots(passages, walls_k):
    pitch = up_to(walls_k * 8, 32)
    per_row = 128 // pitch
    return pitch, per_row, up_to(passages, per_row) // per_row * 128


def constants(layers, passages, walls_k):
    rows = HB * NV * layers
    padded = up_to(rows, 16)
    side = up_to(HB * NV, 16)
    width = padded + 2 * side
    harmonic = harmonic_matrix(HB)
    scale = near_scale(np.unique(np.abs(harmonic[harmonic != 0])))
    mix = np.zeros((padded, padded), np.float32)
    axial = np.zeros((padded, width), np.float32)
    fixed = np.zeros((3, padded, width), np.float32)
    pick = np.zeros((2 * side, padded), np.float32)
    weights = np.zeros((8, padded), np.int32)
    of_row = np.zeros((padded, NV), np.float32)
    of_column = np.zeros((NV, width), np.float32)
    for i in range(rows):
        r, a = divmod(i, layers)
        n, v = divmod(r, NV)
        of_row[i, v] = 1
        of_column[v, i] = 1
        of_column[v, padded + r] = 1
        of_column[v, padded + side + r] = 1
        weights[n, i] = v + 1
        if a == 0:
            pick[r, i] = 1
        if a == layers - 1:
            pick[side + r, i] = 1
        for w in range(NV):
            q = n * NV + w
            mix[i, q * layers + a] = 1
            axial[i, q * layers + a + 1 if a < layers - 1 else padded + q] = 1
            axial[i, q * layers + a - 1 if a > 0 else padded + side + q] = -1
        fixed[1, i, i] = -1
        fixed[1, i, i + 1 if a < layers - 1 else padded + r] = 1
        fixed[2, i, i] = -1
        fixed[2, i, i - 1 if a > 0 else padded + side + r] = 1
        for m in range(HB):
            fixed[0, i, (m * NV + v) * layers + a] = scale * harmonic[n, m]
    modes = np.zeros((up_to(walls_k * passages, 16), 2 * walls_k * passages), np.float32)
    for p in range(passages):
        for d in range(passages):
            angle = 2.0 * math.pi * (d * p % passages) / passages
            for k in range(walls_k):
                modes[p * walls_k + k, k * passages + d] = math.cos(angle)
                modes[p * walls_k + k, (walls_k + k) * passages + d] = -math.sin(angle)
    arrays = (
        mix.astype(BF16),
        axial.astype(BF16),
        fixed.reshape(3 * padded, width).astype(BF16),
        pick.astype(BF16),
        weights,
        of_row.astype(BF16),
        of_column.astype(BF16),
        modes,
    )
    return arrays, scale


def dot(a, b):
    return jnp.dot(a, b, preferred_element_type=F32)


def kernel(
    *refs, n_in, n_cell, n_circ, layers, padded, scale,
):
    sources = refs[:n_in]
    image, modal = refs[n_in : n_in + 2]
    held_in = refs[n_in + 2 : 2 * n_in + 2]
    (
        state, time_coef, axial_damp, plane_damp, periodic_damp, jac, faces, sides, face_map,
        wall_cells, normals, press_w, mode_shapes,
        mix_c, axial_c, fixed_c, pick_c, weights_c, of_row_c, of_column_c, modes_c,
    ) = held_in
    (
        extra, signed, joint, stack, cell_out, above, below, side_out, side_next, side_prev,
        forces, modes_high, modes_low, flux, total,
        cell_send, cell_recv, side_send, side_recv, force_send, force_recv, load_sem,
    ) = refs[2 * n_in + 2 :]
    me_cell = lax.axis_index("cell")
    me_circ = lax.axis_index("circ")
    me = me_circ * n_cell + me_cell

    def cell_at(j):
        return {"cell": lax.rem(me_cell + j, n_cell)}

    def circ_at(j):
        return {"circ": lax.rem(me_circ + j, n_circ)}

    def peer(i, j):
        return {"circ": lax.rem(me_circ + i, n_circ), "cell": lax.rem(me_cell + j, n_cell)}

    peers = [(i % n_circ, j) for i in range(1, n_circ + 1) for j in range(n_cell)][:-n_cell]
    peers += [(0, j) for j in range(1, n_cell)]
    loads = {}

    def fetch(which):
        for at in which:
            loads[at] = pltpu.make_async_copy(sources[at], held_in[at], load_sem.at[at])
            loads[at].start()

    fetch(LOAD_ORDER[:2])
    peers = [(i % n_circ, j) for i in range(1, n_circ + 1) for j in range(n_cell)][:-n_cell]
    peers += [(0, j) for j in range(1, n_cell)]
    barrier = pltpu.get_barrier_semaphore()
    for i, j in peers:
        pl.semaphore_signal(barrier, inc=1, device_id=peer(i, j), device_id_type=MESH)
    fetch(LOAD_ORDER[2:5])

    def load(*which):
        for at in which:
            loads.pop(at).wait()

    n_rows, _, cells = state.shape
    n_faces = faces.shape[1]
    n_walls = wall_cells.shape[1]
    per = sides.shape[1]
    side_rows = above.shape[0]
    walls_k = normals.shape[0]
    groups = padded // 8

    def by_layer(value, pattern):
        return (value.reshape(groups, 8, value.shape[1]) * pattern[None]).reshape(value.shape)

    def pattern_of(rows):
        return jnp.concatenate([rows] * (8 // layers), axis=0)

    def remote(source, target, send_sem, recv_sem, device):
        return pltpu.make_async_remote_copy(
            src_ref=source, dst_ref=target, send_sem=send_sem, recv_sem=recv_sem,
            device_id=device, device_id_type=MESH,
        )

    to_below = remote(
        cell_out.at[pl.ds(0, side_rows)], above, cell_send.at[0], cell_recv.at[0],
        cell_at(n_cell - 1),
    )
    to_above = remote(
        cell_out.at[pl.ds(side_rows, side_rows + 16)], below, cell_send.at[1], cell_recv.at[1],
        cell_at(1),
    )
    to_prev = remote(side_out, side_next, side_send.at[0], side_recv.at[0], circ_at(n_circ - 1))
    to_next = remote(side_out, side_prev, side_send.at[1], side_recv.at[1], circ_at(1))
    copies = [to_below, to_above, to_prev, to_next]

    def send_sides():
        for copy in copies:
            copy.start()

    band = lax.broadcasted_iota(jnp.int32, (GROUP, 128), 0).astype(F32).astype(BF16)
    one = jnp.ones((GROUP, 128), BF16)
    zero = jnp.zeros((GROUP, 128), BF16)

    def spread(row):
        return jnp.broadcast_to(row.astype(F32).astype(BF16), (GROUP, 128))

    def split(row):
        high = lax.shift_right_logical(row, GROUP.bit_length() - 1)
        return spread(high), jnp.where(band == spread(row - high * GROUP), one, zero)

    def mark(columns, first):
        for at in range(0, columns.shape[1], 128):
            high, low = split(columns[:, at : at + 128])
            for h in range(cells // GROUP):
                hit = jnp.where(high == h, low, zero)
                here = slice(first + at, first + at + 128)
                extra[h * GROUP : (h + 1) * GROUP, here] = hit.astype(F8)

    load(WALL_CELLS)
    wall_index = wall_cells[...]
    wall_layer = lax.div(wall_index, cells)
    mark(wall_index - wall_layer * cells, 0)

    load(STATE)
    wide = state[...].astype(F32)
    pieces = [wide[r] for r in range(n_rows)]
    pieces.append(jnp.zeros((padded - n_rows * layers, cells), F32))
    u = jnp.concatenate(pieces, axis=0).astype(BF16)
    stack[0:padded, :] = u

    load(NORMALS, PRESS_W, WEIGHTS_C)
    gathered = dot(u, extra[:, 0:n_walls])
    layer_of = lax.rem(lax.broadcasted_iota(jnp.int32, (8, n_walls), 0), layers)
    here = by_layer(gathered, (layer_of == wall_layer).astype(F32)).astype(BF16)
    weight_class = weights_c[...]
    weight = jnp.zeros(weight_class.shape, F32)
    for v in range(NV):
        weight = jnp.where(weight_class == v + 1, press_w[v], weight)
    high = weight.astype(BF16)
    low = (weight - high.astype(F32)).astype(BF16)
    pressure = dot(high, here) + dot(low, here)
    pitch, per_row, _ = force_slots(n_circ, walls_k)
    lane = lax.broadcasted_iota(jnp.int32, (8, 128), 1)
    lane = lane - lax.broadcasted_iota(jnp.int32, (8, 128), 0) - lax.rem(me_circ, per_row) * pitch
    tile = jnp.zeros((8, 128), F32)
    for k in range(walls_k):
        force = jnp.sum(pressure * normals[k : k + 1, :], axis=1, keepdims=True)
        tile = jnp.where(lane == k * 8, force, tile)
    forces[me] = jnp.sum(tile, axis=0, keepdims=True)

    early = me_circ < n_circ // 4
    late = me_circ >= n_circ - n_circ // 4
    middle = jnp.logical_not(jnp.logical_or(early, late))

    def enter_and_send_forces():
        pl.semaphore_wait(barrier, n_cell * n_circ - 1)
        for i, j in peers:
            remote(forces.at[me], forces.at[me], force_send, force_recv, peer(i, j)).start()

    def enter_and_send_all():
        enter_and_send_forces()
        send_sides()

    pl.when(late)(enter_and_send_forces)
    fetch(LOAD_ORDER[5:])

    load(FACE_MAP, SIDES, PERIODIC_DAMP, AXIAL_DAMP, PICK_C)
    order = face_map[...]
    hits = (lax.broadcasted_iota(jnp.int32, (per, per), 0) == order).astype(F32)
    targets = jnp.dot(sides[0:1, :].astype(F32), hits, precision=HI, preferred_element_type=F32)
    targets = (targets + 0.5).astype(jnp.int32)
    mark(jnp.concatenate([sides[1:2, :], targets], axis=1), n_walls)

    cell_out[0 : 2 * side_rows, :] = dot(pick_c[...], u).astype(BF16)
    damp = axial_damp[0].astype(F32)
    last = damp[layers - 1 : layers]
    cell_out[2 * side_rows :, :] = jnp.broadcast_to(last, (16, cells)).astype(BF16)
    own_side = dot(u, extra[:, n_walls:])
    side_out[0:padded, :] = own_side.astype(BF16)
    side_damp = periodic_damp[0].astype(F32)
    side_pattern = pattern_of(jnp.concatenate([side_damp, side_damp], axis=1))
    side_out[padded:, :] = jnp.concatenate([side_pattern, side_pattern], axis=0).astype(BF16)
    pl.when(late)(send_sides)

    load(JAC, OF_ROW_C, OF_COLUMN_C, MIX_C, AXIAL_C, PLANE_DAMP, FACES)

    def mixing(face, mask):
        values = (0.5 * jac[:, face, :]).astype(BF16)
        across = dot(values, of_column_c[:, : mask.shape[1]]).astype(BF16)
        return (dot(of_row_c[...], across) * mask.astype(F32)).astype(BF16)

    axial_mix = mixing(0, axial_c[...])
    plane_mix = mixing(1, mix_c[...])
    side_mix = mixing(2, mix_c[...])

    convected = dot(plane_mix, u).astype(BF16)
    plane_pattern = pattern_of(0.5 * plane_damp[0].astype(F32))

    def build(first, count):
        for at in range(first, first + count, 128):
            owner_high, owner = split(faces[0:1, at : at + 128])
            other_high, other = split(faces[1:2, at : at + 128])
            same = owner_high == other_high
            both = owner - other
            by_owner = jnp.where(same, both, owner)
            by_other = jnp.where(same, both, -other)
            for h in range(cells // GROUP):
                hit = jnp.where(other_high == h, by_other, zero)
                hit = jnp.where(owner_high == h, by_owner, hit)
                here = slice(h * GROUP, (h + 1) * GROUP)
                signed[here, at : at + 128] = hit.astype(F8)
                joint[here, at : at + 128] = jnp.abs(hit).astype(F8)

    def gather(first, count):
        here = slice(first, first + count)
        damped = by_layer(dot(u, signed[:, here]), plane_pattern[:, here])
        flux[:, here] = (dot(convected, joint[:, here]) + damped).astype(BF16)

    part = 256
    starts = list(range(0, n_faces, part))
    build(0, part)
    for at in starts:
        if at + part < n_faces:
            build(at + part, part)
        gather(at, part)
        if at == starts[len(starts) // 2 - 1]:
            pl.when(middle)(enter_and_send_all)

    load(MODE_SHAPES, MODES_C)
    shapes = mode_shapes[...].reshape(2 * walls_k * n_circ, mode_shapes.shape[3])
    by_passage = jnp.dot(modes_c[...], shapes, precision=HI, preferred_element_type=F32)
    modes_high[...] = jnp.zeros(modes_high.shape, BF16)
    modes_low[...] = jnp.zeros(modes_low.shape, BF16)
    for p in range(n_circ):
        first = p // per_row * 128 + p % per_row * pitch
        rows = [by_passage[p * walls_k + k : p * walls_k + k + 1] for k in range(walls_k)]
        rows = [jnp.broadcast_to(row, (8, row.shape[1])) for row in rows]
        rows += [jnp.zeros_like(rows[0])] * (pitch // 8 - walls_k)
        rows = jnp.concatenate(rows, axis=0)
        high = rows.astype(BF16)
        modes_high[first : first + pitch, :] = high
        modes_low[first : first + pitch, :] = (rows - high.astype(F32)).astype(BF16)

    total[...] = lax.dot_general(
        flux[...], signed[...], NT, preferred_element_type=F32
    )

    pl.when(early)(enter_and_send_all)

    to_below.wait_recv()
    to_above.wait_recv()
    load(FIXED_C, TIME_COEF)
    above_rows = above[...].astype(F32)
    stack[padded : padded + side_rows, :] = jnp.where(
        me_cell == n_cell - 1, 0.0, above_rows
    ).astype(BF16)
    below_rows = below[0:side_rows, :].astype(F32)
    stack[padded + side_rows :, :] = jnp.where(
        me_cell == 0, -cell_out[0:side_rows, :].astype(F32), below_rows
    ).astype(BF16)
    below_damp = below[side_rows : side_rows + 16, :].astype(F32)[0:1]
    below_damp = jnp.where(me_cell == 0, 0.0, below_damp)
    held = stack[...]
    derived = dot(fixed_c[...], held)
    result = by_layer(derived[0:padded], pattern_of(time_coef[0] * (1.0 / scale)))
    result = result - by_layer(derived[padded : 2 * padded], pattern_of(0.5 * damp))
    lower_damp = jnp.concatenate([below_damp, damp[0 : layers - 1]], axis=0)
    result = result - by_layer(derived[2 * padded :], pattern_of(0.5 * lower_damp))
    result = result + dot(axial_mix, held)

    to_prev.wait_recv()
    to_next.wait_recv()
    left = lax.broadcasted_iota(jnp.int32, (padded, 2 * per), 1) < per
    ahead = pltpu.roll(side_next[0:padded, :].astype(F32), per, 1)
    back = pltpu.roll(side_prev[0:padded, :].astype(F32), per, 1)
    back_damp = side_prev[padded:, :].astype(F32)[0:8]
    lower = jnp.where(left, own_side, back)
    upper = jnp.where(left, ahead, own_side)
    side_s = 0.5 * jnp.where(left[0:8], side_pattern, back_damp)
    lower_b, upper_b = lower.astype(BF16), upper.astype(BF16)
    side_flux = dot(side_mix, lower_b) + dot(side_mix, upper_b)
    side_flux = side_flux - by_layer(upper - lower, side_s)
    side_flux = jnp.where(left, side_flux, -side_flux).astype(BF16)
    result = result + lax.dot_general(
        side_flux, extra[:, n_walls:], NT, preferred_element_type=F32
    )
    result = result + total[...]
    for r in range(n_rows):
        image[r] = result[r * layers : (r + 1) * layers].astype(BF16)

    others = n_cell * n_circ - 1
    arrived = pltpu.make_async_remote_copy(
        src_ref=forces.at[pl.ds(0, others)], dst_ref=forces.at[pl.ds(0, others)],
        send_sem=force_send, recv_sem=force_recv, device_id=peer(0, 1), device_id_type=MESH,
    )
    arrived.wait_recv()
    sublane = lax.broadcasted_iota(jnp.int32, (8, 128), 0)
    kept = lax.rem(lax.broadcasted_iota(jnp.int32, (8, 128), 1), 8) == sublane
    rows = []
    for first in range(0, n_circ, per_row):
        slots = range(first * n_cell, min(first + per_row, n_circ) * n_cell)
        row = [forces[slot] for slot in slots]
        while len(row) > 1:
            row = [a + b for a, b in zip(row[::2], row[1::2])] + row[len(row) // 2 * 2 :]
        rows.append(jnp.where(kept, jnp.broadcast_to(row[0], (8, 128)), 0.0))
    every = jnp.concatenate(rows, axis=1)
    high = every.astype(BF16)
    low = (every - high.astype(F32)).astype(BF16)
    table = modes_high[...]
    answer = dot(high, table) + dot(low, table) + dot(high, modes_low[...])
    modal[...] = answer[0:HB]
    arrived.wait_send()
    for copy in copies:
        copy.wait_send()


def deliver(image, modal, image_out, modal_out, sems):
    copies = [
        pltpu.make_async_copy(image, image_out, sems.at[0]),
        pltpu.make_async_copy(modal, modal_out, sems.at[1]),
    ]
    for copy in copies:
        copy.start()
    for copy in copies:
        copy.wait()


def shards(
    flow_state, time_coef, axial_damp, plane_damp, periodic_damp, flux_jacobian, face_cells,
    periodic_cells, face_map, wall_cells, wall_normals, pressure_weights, mode_shapes,
):
    layers, cells = flow_state.shape[2:]
    n_cell = lax.axis_size("cell")
    n_circ = lax.axis_size("circ")
    walls_k = wall_normals.shape[0]
    n_modes = mode_shapes.shape[3]
    per = face_map.shape[0]
    n_faces = face_cells.shape[1]
    n_walls = wall_cells.shape[0]
    fixed, scale = constants(layers, n_circ, walls_k)
    padded = fixed[0].shape[0]
    side = fixed[3].shape[0] // 2
    lanes = force_slots(n_circ, walls_k)[2]
    state = flow_state.reshape(HB * NV, layers, cells)
    vmem = pl.BlockSpec(memory_space=pltpu.VMEM)
    dma = pltpu.SemaphoreType.DMA
    operands = (
        state, time_coef, axial_damp, plane_damp, periodic_damp,
        flux_jacobian.transpose(1, 0, 2), face_cells, periodic_cells, face_map[None],
        wall_cells[None], wall_normals, pressure_weights,
        mode_shapes.transpose(0, 2, 1, 3), *(jnp.asarray(array) for array in fixed),
    )
    hbm = pl.BlockSpec(memory_space=pltpu.HBM)
    held = [
        (pltpu.SMEM if at == PRESS_W else pltpu.VMEM)(array.shape, array.dtype)
        for at, array in enumerate(operands)
    ]
    image, modal = pl.pallas_call(
        functools.partial(
            kernel, n_in=len(operands), n_cell=n_cell, n_circ=n_circ, layers=layers,
            padded=padded, scale=scale,
        ),
        out_shape=(
            jax.ShapeDtypeStruct((HB * NV, layers, cells), BF16),
            jax.ShapeDtypeStruct((HB, n_modes), F32),
        ),
        in_specs=[hbm] * len(operands),
        out_specs=(vmem, vmem),
        scratch_shapes=[
            *held,
            pltpu.VMEM((cells, n_walls + 2 * per), F8),
            pltpu.VMEM((cells, n_faces), F8),
            pltpu.VMEM((cells, n_faces), F8),
            pltpu.VMEM((padded + 2 * side, cells), BF16),
            pltpu.VMEM((2 * side + 16, cells), BF16),
            pltpu.VMEM((side, cells), BF16),
            pltpu.VMEM((side + 16, cells), BF16),
            pltpu.VMEM((padded + 16, 2 * per), BF16),
            pltpu.VMEM((padded + 16, 2 * per), BF16),
            pltpu.VMEM((padded + 16, 2 * per), BF16),
            pltpu.VMEM((n_circ * n_cell, 1, 128), F32),
            pltpu.VMEM((lanes, n_modes), BF16),
            pltpu.VMEM((lanes, n_modes), BF16),
            pltpu.VMEM((padded, n_faces), BF16),
            pltpu.VMEM((padded, cells), F32),
            dma((2,)), dma((2,)), dma((2,)), dma((2,)), dma, dma, dma((len(operands),)),
        ],
        compiler_params=pltpu.CompilerParams(
            collective_id=0, has_side_effects=True, vmem_limit_bytes=VMEM_LIMIT
        ),
    )(*(pltpu.with_memory_space_constraint(array, pltpu.HBM) for array in operands))
    image, modal = pl.pallas_call(
        deliver,
        out_shape=(
            jax.ShapeDtypeStruct(image.shape, BF16),
            jax.ShapeDtypeStruct(modal.shape, F32),
        ),
        in_specs=[vmem] * 2,
        out_specs=(hbm, hbm),
        scratch_shapes=[dma((2,))],
        compiler_params=pltpu.CompilerParams(vmem_limit_bytes=VMEM_LIMIT),
    )(image, modal)
    return image.reshape(HB * NV, 1, layers, cells), modal


def solution(mesh):
    circ = P("circ", "cell", None)
    placed = (
        P(None, "circ", "cell", None), circ, circ, circ, circ, P(), P(), P(), P(),
        P("cell"), P(None, "cell"), P(), P(),
    )
    return jax.shard_map(
        shards,
        mesh=mesh,
        in_specs=placed,
        out_specs=(P(None, "circ", "cell", None), P()),
        check_vma=False,
    )
```

```python
import functools
import math

import jax
import jax.numpy as jnp
import numpy as np
from jax import lax
from jax.experimental import pallas as pl
from jax.experimental.pallas import tpu as pltpu
from jax.sharding import PartitionSpec as P

NV = 5
HB = 7
F32 = jnp.float32
BF16 = jnp.bfloat16
F8 = jnp.float8_e4m3fn
GROUP = 32
VMEM_LIMIT = 24 << 20
(
    STATE, TIME_COEF, AXIAL_DAMP, PLANE_DAMP, PERIODIC_DAMP, JAC, FACES, SIDES, FACE_MAP,
    WALL_CELLS, NORMALS, PRESS_W, MODE_SHAPES,
    MIX_C, AXIAL_C, FIXED_C, PICK_C, WEIGHTS_C, OF_ROW_C, OF_COLUMN_C, MODES_C,
) = range(21)
LOAD_ORDER = (
    STATE, WALL_CELLS, NORMALS, PRESS_W, WEIGHTS_C, FACE_MAP, SIDES, PERIODIC_DAMP, AXIAL_DAMP,
    PICK_C, JAC, OF_ROW_C, OF_COLUMN_C, MIX_C, AXIAL_C, PLANE_DAMP, FACES, MODE_SHAPES, MODES_C,
    FIXED_C, TIME_COEF,
)
HI = lax.Precision.HIGHEST
MESH = pl.DeviceIdType.MESH
NT = (((1,), (1,)), ((), ()))


def up_to(value, step):
    return -(-value // step) * step


def harmonic_matrix(instances):
    matrix = np.zeros((instances, instances))
    for n in range(instances):
        for m in range(instances):
            if n != m:
                matrix[n, m] = 0.5 * (-1.0) ** (n - m) / math.sin(math.pi * (n - m) / instances)
    return matrix


def near_scale(values):
    scales = 1.0 + np.arange(4096) / 4096.0
    scaled = scales[:, None] * values[None, :]
    rounded = scaled.astype(BF16).astype(np.float64)
    return float(scales[np.argmin(np.max(np.abs(rounded / scaled - 1.0), axis=1))])


def force_slots(passages, walls_k):
    pitch = up_to(walls_k * 8, 32)
    per_row = 128 // pitch
    return pitch, per_row, up_to(passages, per_row) // per_row * 128


def constants(layers, passages, walls_k):
    rows = HB * NV * layers
    padded = up_to(rows, 16)
    side = up_to(HB * NV, 16)
    width = padded + 2 * side
    harmonic = harmonic_matrix(HB)
    scale = near_scale(np.unique(np.abs(harmonic[harmonic != 0])))
    mix = np.zeros((padded, padded), np.float32)
    axial = np.zeros((padded, width), np.float32)
    fixed = np.zeros((3, padded, width), np.float32)
    pick = np.zeros((2 * side, padded), np.float32)
    weights = np.zeros((8, padded), np.int32)
    of_row = np.zeros((padded, NV), np.float32)
    of_column = np.zeros((NV, width), np.float32)
    for i in range(rows):
        r, a = divmod(i, layers)
        n, v = divmod(r, NV)
        of_row[i, v] = 1
        of_column[v, i] = 1
        of_column[v, padded + r] = 1
        of_column[v, padded + side + r] = 1
        weights[n, i] = v + 1
        if a == 0:
            pick[r, i] = 1
        if a == layers - 1:
            pick[side + r, i] = 1
        for w in range(NV):
            q = n * NV + w
            mix[i, q * layers + a] = 1
            axial[i, q * layers + a + 1 if a < layers - 1 else padded + q] = 1
            axial[i, q * layers + a - 1 if a > 0 else padded + side + q] = -1
        fixed[1, i, i] = -1
        fixed[1, i, i + 1 if a < layers - 1 else padded + r] = 1
        fixed[2, i, i] = -1
        fixed[2, i, i - 1 if a > 0 else padded + side + r] = 1
        for m in range(HB):
            fixed[0, i, (m * NV + v) * layers + a] = scale * harmonic[n, m]
    modes = np.zeros((up_to(walls_k * passages, 16), 2 * walls_k * passages), np.float32)
    for p in range(passages):
        for d in range(passages):
            angle = 2.0 * math.pi * (d * p % passages) / passages
            for k in range(walls_k):
                modes[p * walls_k + k, k * passages + d] = math.cos(angle)
                modes[p * walls_k + k, (walls_k + k) * passages + d] = -math.sin(angle)
    arrays = (
        mix.astype(BF16),
        axial.astype(BF16),
        fixed.reshape(3 * padded, width).astype(BF16),
        pick.astype(BF16),
        weights,
        of_row.astype(BF16),
        of_column.astype(BF16),
        modes,
    )
    return arrays, scale


def dot(a, b):
    return jnp.dot(a, b, preferred_element_type=F32)


def kernel(
    *refs, n_in, n_cell, n_circ, layers, padded, scale,
):
    sources = refs[:n_in]
    image, modal = refs[n_in : n_in + 2]
    held_in = refs[n_in + 2 : 2 * n_in + 2]
    (
        state, time_coef, axial_damp, plane_damp, periodic_damp, jac, faces, sides, face_map,
        wall_cells, normals, press_w, mode_shapes,
        mix_c, axial_c, fixed_c, pick_c, weights_c, of_row_c, of_column_c, modes_c,
    ) = held_in
    (
        extra, signed, joint, stack, cell_out, above, below, side_out, side_next, side_prev,
        forces, modes_high, modes_low, flux, total,
        cell_send, cell_recv, side_send, side_recv, force_send, force_recv, load_sem,
    ) = refs[2 * n_in + 2 :]
    me_cell = lax.axis_index("cell")
    me_circ = lax.axis_index("circ")
    me = me_circ * n_cell + me_cell

    def cell_at(j):
        return {"cell": lax.rem(me_cell + j, n_cell)}

    def circ_at(j):
        return {"circ": lax.rem(me_circ + j, n_circ)}

    def peer(i, j):
        return {"circ": lax.rem(me_circ + i, n_circ), "cell": lax.rem(me_cell + j, n_cell)}

    peers = [(i % n_circ, j) for i in range(1, n_circ + 1) for j in range(n_cell)][:-n_cell]
    peers += [(0, j) for j in range(1, n_cell)]
    loads = {}

    def fetch(which):
        for at in which:
            loads[at] = pltpu.make_async_copy(sources[at], held_in[at], load_sem.at[at])
            loads[at].start()

    fetch(LOAD_ORDER[:2])
    peers = [(i % n_circ, j) for i in range(1, n_circ + 1) for j in range(n_cell)][:-n_cell]
    peers += [(0, j) for j in range(1, n_cell)]
    barrier = pltpu.get_barrier_semaphore()
    for i, j in peers:
        pl.semaphore_signal(barrier, inc=1, device_id=peer(i, j), device_id_type=MESH)
    fetch(LOAD_ORDER[2:])

    def load(*which):
        for at in which:
            loads.pop(at).wait()

    n_rows, _, cells = state.shape
    n_faces = faces.shape[1]
    n_walls = wall_cells.shape[1]
    per = sides.shape[1]
    side_rows = above.shape[0]
    walls_k = normals.shape[0]
    groups = padded // 8

    def by_layer(value, pattern):
        return (value.reshape(groups, 8, value.shape[1]) * pattern[None]).reshape(value.shape)

    def pattern_of(rows):
        return jnp.concatenate([rows] * (8 // layers), axis=0)

    def remote(source, target, send_sem, recv_sem, device):
        return pltpu.make_async_remote_copy(
            src_ref=source, dst_ref=target, send_sem=send_sem, recv_sem=recv_sem,
            device_id=device, device_id_type=MESH,
        )

    to_below = remote(
        cell_out.at[pl.ds(0, side_rows)], above, cell_send.at[0], cell_recv.at[0],
        cell_at(n_cell - 1),
    )
    to_above = remote(
        cell_out.at[pl.ds(side_rows, side_rows)], below, cell_send.at[1], cell_recv.at[1],
        cell_at(1),
    )
    to_prev = remote(
        side_out.at[0], side_next, side_send.at[0], side_recv.at[0], circ_at(n_circ - 1)
    )
    to_next = remote(side_out.at[1], side_prev, side_send.at[1], side_recv.at[1], circ_at(1))
    has_below = me_cell > 0
    has_above = me_cell < n_cell - 1

    def send_sides():
        to_prev.start()
        to_next.start()
        pl.when(has_above)(to_above.start)
        pl.when(has_below)(to_below.start)

    band = lax.broadcasted_iota(jnp.int32, (GROUP, 128), 0).astype(F32).astype(BF16)
    one = jnp.ones((GROUP, 128), BF16)
    zero = jnp.zeros((GROUP, 128), BF16)

    def spread(row):
        return jnp.broadcast_to(row.astype(F32).astype(BF16), (GROUP, 128))

    def split(row):
        high = lax.shift_right_logical(row, GROUP.bit_length() - 1)
        return spread(high), jnp.where(band == spread(row - high * GROUP), one, zero)

    def mark(columns, first):
        for at in range(0, columns.shape[1], 128):
            high, low = split(columns[:, at : at + 128])
            for h in range(cells // GROUP):
                hit = jnp.where(high == h, low, zero)
                here = slice(first + at, first + at + 128)
                extra[h * GROUP : (h + 1) * GROUP, here] = hit.astype(F8)

    load(WALL_CELLS)
    wall_index = wall_cells[...]
    wall_layer = lax.div(wall_index, cells)
    mark(wall_index - wall_layer * cells, 0)

    load(STATE)
    wide = state[...].astype(F32)
    pieces = [wide[r] for r in range(n_rows)]
    pieces.append(jnp.zeros((padded - n_rows * layers, cells), F32))
    u = jnp.concatenate(pieces, axis=0).astype(BF16)
    stack[0:padded, :] = u

    load(NORMALS, PRESS_W, WEIGHTS_C)
    gathered = dot(u, extra[:, 0:n_walls])
    layer_of = lax.rem(lax.broadcasted_iota(jnp.int32, (8, n_walls), 0), layers)
    here = by_layer(gathered, (layer_of == wall_layer).astype(F32)).astype(BF16)
    weight_class = weights_c[...]
    weight = jnp.zeros(weight_class.shape, F32)
    for v in range(NV):
        weight = jnp.where(weight_class == v + 1, press_w[v], weight)
    high = weight.astype(BF16)
    low = (weight - high.astype(F32)).astype(BF16)
    pressure = dot(high, here) + dot(low, here)
    pitch, per_row, _ = force_slots(n_circ, walls_k)
    lane = lax.broadcasted_iota(jnp.int32, (8, 128), 1)
    lane = lane - lax.broadcasted_iota(jnp.int32, (8, 128), 0) - lax.rem(me_circ, per_row) * pitch
    tile = jnp.zeros((8, 128), F32)
    for k in range(walls_k):
        force = jnp.sum(pressure * normals[k : k + 1, :], axis=1, keepdims=True)
        tile = jnp.where(lane == k * 8, force, tile)
    forces[me] = jnp.sum(tile, axis=0, keepdims=True)

    early = me_circ < n_circ // 4
    late = me_circ >= n_circ - n_circ // 4
    middle = jnp.logical_not(jnp.logical_or(early, late))

    def enter_and_send_forces():
        pl.semaphore_wait(barrier, n_cell * n_circ - 1)
        for i, j in peers:
            remote(forces.at[me], forces.at[me], force_send, force_recv, peer(i, j)).start()

    def enter_and_send_all():
        enter_and_send_forces()
        send_sides()

    pl.when(late)(enter_and_send_forces)

    load(FACE_MAP, SIDES, PERIODIC_DAMP, AXIAL_DAMP, PICK_C)
    order = face_map[...]
    hits = (lax.broadcasted_iota(jnp.int32, (per, per), 0) == order).astype(F32)
    targets = jnp.dot(sides[0:1, :].astype(F32), hits, precision=HI, preferred_element_type=F32)
    targets = (targets + 0.5).astype(jnp.int32)
    mark(jnp.concatenate([sides[1:2, :], targets], axis=1), n_walls)

    own_side = dot(u, extra[:, n_walls:])
    side_damp = periodic_damp[0].astype(F32)
    side_pattern = pattern_of(jnp.concatenate([side_damp, side_damp], axis=1))
    half = padded // 2
    left = lax.broadcasted_iota(jnp.int32, (half, 2 * per), 1) < per
    first_half, second_half = own_side[0:half], own_side[half:]
    filler = [side_pattern] * ((side_out.shape[1] - half) // 8)
    lower_own = jnp.where(left, pltpu.roll(first_half, per, 1), second_half)
    upper_own = jnp.where(left, first_half, pltpu.roll(second_half, per, 1))
    side_out[0] = jnp.concatenate([lower_own, *filler], axis=0).astype(BF16)
    side_out[1] = jnp.concatenate([upper_own, *filler], axis=0).astype(BF16)

    damp = axial_damp[0].astype(F32)
    last = damp[layers - 1 : layers]
    picked = dot(pick_c[...], u)
    spare = lax.broadcasted_iota(jnp.int32, (16, cells), 0) == 15
    tail = jnp.where(spare, jnp.broadcast_to(last, (16, cells)), picked[2 * side_rows - 16 :])
    cell_out[0 : 2 * side_rows - 16, :] = picked[0 : 2 * side_rows - 16].astype(BF16)
    cell_out[2 * side_rows - 16 :, :] = tail.astype(BF16)

    pl.when(late)(send_sides)

    load(JAC, OF_ROW_C, OF_COLUMN_C, MIX_C, AXIAL_C, PLANE_DAMP, FACES)

    def mixing(face, mask):
        values = (0.5 * jac[:, face, :]).astype(BF16)
        across = dot(values, of_column_c[:, : mask.shape[1]]).astype(BF16)
        return (dot(of_row_c[...], across) * mask.astype(F32)).astype(BF16)

    axial_mix = mixing(0, axial_c[...])
    plane_mix = mixing(1, mix_c[...])
    side_mix = mixing(2, mix_c[...])

    convected = dot(plane_mix, u).astype(BF16)
    plane_pattern = pattern_of(0.5 * plane_damp[0].astype(F32))

    def build(first, count):
        for at in range(first, first + count, 128):
            owner_high, owner = split(faces[0:1, at : at + 128])
            other_high, other = split(faces[1:2, at : at + 128])
            same = owner_high == other_high
            both = owner - other
            by_owner = jnp.where(same, both, owner)
            by_other = jnp.where(same, both, -other)
            for h in range(cells // GROUP):
                hit = jnp.where(other_high == h, by_other, zero)
                hit = jnp.where(owner_high == h, by_owner, hit)
                here = slice(h * GROUP, (h + 1) * GROUP)
                signed[here, at : at + 128] = hit.astype(F8)
                joint[here, at : at + 128] = jnp.abs(hit).astype(F8)

    def gather(first, count):
        here = slice(first, first + count)
        damped = by_layer(dot(u, signed[:, here]), plane_pattern[:, here])
        flux[:, here] = (dot(convected, joint[:, here]) + damped).astype(BF16)

    part = 256
    starts = list(range(0, n_faces, part))
    build(0, part)
    for at in starts:
        if at + part < n_faces:
            build(at + part, part)
        gather(at, part)
        if at == starts[len(starts) // 2 - 1]:
            pl.when(middle)(enter_and_send_all)

    load(MODE_SHAPES, MODES_C)
    shapes = mode_shapes[...].reshape(2 * walls_k * n_circ, mode_shapes.shape[3])
    by_passage = jnp.dot(modes_c[...], shapes, precision=HI, preferred_element_type=F32)
    modes_high[...] = jnp.zeros(modes_high.shape, BF16)
    modes_low[...] = jnp.zeros(modes_low.shape, BF16)
    for p in range(n_circ):
        first = p // per_row * 128 + p % per_row * pitch
        rows = [by_passage[p * walls_k + k : p * walls_k + k + 1] for k in range(walls_k)]
        rows = [jnp.broadcast_to(row, (8, row.shape[1])) for row in rows]
        rows += [jnp.zeros_like(rows[0])] * (pitch // 8 - walls_k)
        rows = jnp.concatenate(rows, axis=0)
        high = rows.astype(BF16)
        modes_high[first : first + pitch, :] = high
        modes_low[first : first + pitch, :] = (rows - high.astype(F32)).astype(BF16)

    total[...] = lax.dot_general(
        flux[...], signed[...], NT, preferred_element_type=F32
    )

    pl.when(early)(enter_and_send_all)

    pl.when(has_above)(to_below.wait_recv)
    pl.when(has_below)(to_above.wait_recv)
    load(FIXED_C, TIME_COEF)
    above_rows = above[...].astype(F32)
    stack[padded : padded + side_rows, :] = jnp.where(
        me_cell == n_cell - 1, 0.0, above_rows
    ).astype(BF16)
    below_rows = below[...].astype(F32)
    stack[padded + side_rows :, :] = jnp.where(
        me_cell == 0, -cell_out[0:side_rows, :].astype(F32), below_rows
    ).astype(BF16)
    below_damp = below[side_rows - 16 : side_rows, :].astype(F32)[15:16]
    below_damp = jnp.where(me_cell == 0, 0.0, below_damp)
    held = stack[...]
    derived = dot(fixed_c[...], held)
    result = by_layer(derived[0:padded], pattern_of(time_coef[0] * (1.0 / scale)))
    result = result - by_layer(derived[padded : 2 * padded], pattern_of(0.5 * damp))
    lower_damp = jnp.concatenate([below_damp, damp[0 : layers - 1]], axis=0)
    result = result - by_layer(derived[2 * padded :], pattern_of(0.5 * lower_damp))
    result = result + dot(axial_mix, held)

    to_prev.wait_recv()
    to_next.wait_recv()
    ahead = side_next[0:half, :].astype(F32)
    back = side_prev[0:half, :].astype(F32)
    back_damp = side_prev[half:, :].astype(F32)[0:8]
    ahead = jnp.concatenate([ahead, pltpu.roll(ahead, per, 1)], axis=0)
    back = jnp.concatenate([pltpu.roll(back, per, 1), back], axis=0)
    left = jnp.concatenate([left, left], axis=0)
    lower = jnp.where(left, own_side, back)
    upper = jnp.where(left, ahead, own_side)
    side_s = 0.5 * jnp.where(left[0:8], side_pattern, back_damp)
    lower_b, upper_b = lower.astype(BF16), upper.astype(BF16)
    side_flux = dot(side_mix, lower_b) + dot(side_mix, upper_b)
    side_flux = side_flux - by_layer(upper - lower, side_s)
    side_flux = jnp.where(left, side_flux, -side_flux).astype(BF16)
    result = result + lax.dot_general(
        side_flux, extra[:, n_walls:], NT, preferred_element_type=F32
    )
    result = result + total[...]
    for r in range(n_rows):
        image[r] = result[r * layers : (r + 1) * layers].astype(BF16)

    others = n_cell * n_circ - 1
    arrived = pltpu.make_async_remote_copy(
        src_ref=forces.at[pl.ds(0, others)], dst_ref=forces.at[pl.ds(0, others)],
        send_sem=force_send, recv_sem=force_recv, device_id=peer(0, 1), device_id_type=MESH,
    )
    arrived.wait_recv()
    sublane = lax.broadcasted_iota(jnp.int32, (8, 128), 0)
    kept = lax.rem(lax.broadcasted_iota(jnp.int32, (8, 128), 1), 8) == sublane
    rows = []
    for first in range(0, n_circ, per_row):
        slots = range(first * n_cell, min(first + per_row, n_circ) * n_cell)
        row = [forces[slot] for slot in slots]
        while len(row) > 1:
            row = [a + b for a, b in zip(row[::2], row[1::2])] + row[len(row) // 2 * 2 :]
        rows.append(jnp.where(kept, jnp.broadcast_to(row[0], (8, 128)), 0.0))
    every = jnp.concatenate(rows, axis=1)
    high = every.astype(BF16)
    low = (every - high.astype(F32)).astype(BF16)
    table = modes_high[...]
    answer = dot(high, table) + dot(low, table) + dot(high, modes_low[...])
    modal[...] = answer[0:HB]
    arrived.wait_send()
    to_prev.wait_send()
    to_next.wait_send()
    pl.when(has_above)(to_above.wait_send)
    pl.when(has_below)(to_below.wait_send)


def deliver(image, modal, image_out, modal_out, sems):
    copies = [
        pltpu.make_async_copy(image, image_out, sems.at[0]),
        pltpu.make_async_copy(modal, modal_out, sems.at[1]),
    ]
    for copy in copies:
        copy.start()
    for copy in copies:
        copy.wait()


def shards(
    flow_state, time_coef, axial_damp, plane_damp, periodic_damp, flux_jacobian, face_cells,
    periodic_cells, face_map, wall_cells, wall_normals, pressure_weights, mode_shapes,
):
    layers, cells = flow_state.shape[2:]
    n_cell = lax.axis_size("cell")
    n_circ = lax.axis_size("circ")
    walls_k = wall_normals.shape[0]
    n_modes = mode_shapes.shape[3]
    per = face_map.shape[0]
    n_faces = face_cells.shape[1]
    n_walls = wall_cells.shape[0]
    fixed, scale = constants(layers, n_circ, walls_k)
    padded = fixed[0].shape[0]
    side = fixed[3].shape[0] // 2
    lanes = force_slots(n_circ, walls_k)[2]
    packed = up_to(padded // 2 + 8, 16)
    state = flow_state.reshape(HB * NV, layers, cells)
    vmem = pl.BlockSpec(memory_space=pltpu.VMEM)
    dma = pltpu.SemaphoreType.DMA
    operands = (
        state, time_coef, axial_damp, plane_damp, periodic_damp,
        flux_jacobian.transpose(1, 0, 2), face_cells, periodic_cells, face_map[None],
        wall_cells[None], wall_normals, pressure_weights,
        mode_shapes.transpose(0, 2, 1, 3), *(jnp.asarray(array) for array in fixed),
    )
    hbm = pl.BlockSpec(memory_space=pltpu.HBM)
    held = [
        (pltpu.SMEM if at == PRESS_W else pltpu.VMEM)(array.shape, array.dtype)
        for at, array in enumerate(operands)
    ]
    image, modal = pl.pallas_call(
        functools.partial(
            kernel, n_in=len(operands), n_cell=n_cell, n_circ=n_circ, layers=layers,
            padded=padded, scale=scale,
        ),
        out_shape=(
            jax.ShapeDtypeStruct((HB * NV, layers, cells), BF16),
            jax.ShapeDtypeStruct((HB, n_modes), F32),
        ),
        in_specs=[hbm] * len(operands),
        out_specs=(vmem, vmem),
        scratch_shapes=[
            *held,
            pltpu.VMEM((cells, n_walls + 2 * per), F8),
            pltpu.VMEM((cells, n_faces), F8),
            pltpu.VMEM((cells, n_faces), F8),
            pltpu.VMEM((padded + 2 * side, cells), BF16),
            pltpu.VMEM((2 * side, cells), BF16),
            pltpu.VMEM((side, cells), BF16),
            pltpu.VMEM((side, cells), BF16),
            pltpu.VMEM((2, packed, 2 * per), BF16),
            pltpu.VMEM((packed, 2 * per), BF16),
            pltpu.VMEM((packed, 2 * per), BF16),
            pltpu.VMEM((n_circ * n_cell, 1, 128), F32),
            pltpu.VMEM((lanes, n_modes), BF16),
            pltpu.VMEM((lanes, n_modes), BF16),
            pltpu.VMEM((padded, n_faces), BF16),
            pltpu.VMEM((padded, cells), F32),
            dma((2,)), dma((2,)), dma((2,)), dma((2,)), dma, dma, dma((len(operands),)),
        ],
        compiler_params=pltpu.CompilerParams(
            collective_id=0, has_side_effects=True, vmem_limit_bytes=VMEM_LIMIT
        ),
    )(*(pltpu.with_memory_space_constraint(array, pltpu.HBM) for array in operands))
    image, modal = pl.pallas_call(
        deliver,
        out_shape=(
            jax.ShapeDtypeStruct(image.shape, BF16),
            jax.ShapeDtypeStruct(modal.shape, F32),
        ),
        in_specs=[vmem] * 2,
        out_specs=(hbm, hbm),
        scratch_shapes=[dma((2,))],
        compiler_params=pltpu.CompilerParams(vmem_limit_bytes=VMEM_LIMIT),
    )(image, modal)
    return image.reshape(HB * NV, 1, layers, cells), modal


def solution(mesh):
    circ = P("circ", "cell", None)
    placed = (
        P(None, "circ", "cell", None), circ, circ, circ, circ, P(), P(), P(), P(),
        P("cell"), P(None, "cell"), P(), P(),
    )
    return jax.shard_map(
        shards,
        mesh=mesh,
        in_specs=placed,
        out_specs=(P(None, "circ", "cell", None), P()),
        check_vma=False,
    )
```

```python
import functools
import math

import jax
import jax.numpy as jnp
import numpy as np
from jax import lax
from jax.experimental import pallas as pl
from jax.experimental.pallas import tpu as pltpu
from jax.sharding import PartitionSpec as P

NV = 5
HB = 7
F32 = jnp.float32
BF16 = jnp.bfloat16
F8 = jnp.float8_e4m3fn
GROUP = 32
VMEM_LIMIT = 24 << 20
(
    STATE, TIME_COEF, AXIAL_DAMP, PLANE_DAMP, PERIODIC_DAMP, JAC, FACES, SIDES, FACE_MAP,
    WALL_CELLS, NORMALS, PRESS_W, MODE_SHAPES,
    MIX_C, AXIAL_C, FIXED_C, PICK_C, WEIGHTS_C, OF_ROW_C, OF_COLUMN_C, MODES_C,
) = range(21)
LOAD_ORDER = (
    STATE, WALL_CELLS, NORMALS, PRESS_W, WEIGHTS_C, FACE_MAP, SIDES, PERIODIC_DAMP, AXIAL_DAMP,
    PICK_C, JAC, OF_ROW_C, OF_COLUMN_C, MIX_C, AXIAL_C, PLANE_DAMP, FACES, MODE_SHAPES, MODES_C,
    FIXED_C, TIME_COEF,
)
HI = lax.Precision.HIGHEST
MESH = pl.DeviceIdType.MESH
NT = (((1,), (1,)), ((), ()))


def up_to(value, step):
    return -(-value // step) * step


def harmonic_matrix(instances):
    matrix = np.zeros((instances, instances))
    for n in range(instances):
        for m in range(instances):
            if n != m:
                matrix[n, m] = 0.5 * (-1.0) ** (n - m) / math.sin(math.pi * (n - m) / instances)
    return matrix


def near_scale(values):
    scales = 1.0 + np.arange(4096) / 4096.0
    scaled = scales[:, None] * values[None, :]
    rounded = scaled.astype(BF16).astype(np.float64)
    return float(scales[np.argmin(np.max(np.abs(rounded / scaled - 1.0), axis=1))])


def force_slots(passages, walls_k):
    pitch = up_to(walls_k * 8, 32)
    per_row = 128 // pitch
    return pitch, per_row, up_to(passages, per_row) // per_row * 128


def constants(layers, passages, walls_k):
    rows = HB * NV * layers
    padded = up_to(rows, 16)
    side = up_to(HB * NV, 16)
    width = padded + 2 * side
    harmonic = harmonic_matrix(HB)
    scale = near_scale(np.unique(np.abs(harmonic[harmonic != 0])))
    mix = np.zeros((padded, padded), np.float32)
    axial = np.zeros((padded, width), np.float32)
    fixed = np.zeros((3, padded, width), np.float32)
    pick = np.zeros((2 * side, padded), np.float32)
    weights = np.zeros((8, padded), np.int32)
    of_row = np.zeros((padded, NV), np.float32)
    of_column = np.zeros((NV, width), np.float32)
    for i in range(rows):
        r, a = divmod(i, layers)
        n, v = divmod(r, NV)
        of_row[i, v] = 1
        of_column[v, i] = 1
        of_column[v, padded + r] = 1
        of_column[v, padded + side + r] = 1
        weights[n, i] = v + 1
        if a == 0:
            pick[r, i] = 1
        if a == layers - 1:
            pick[side + r, i] = 1
        for w in range(NV):
            q = n * NV + w
            mix[i, q * layers + a] = 1
            axial[i, q * layers + a + 1 if a < layers - 1 else padded + q] = 1
            axial[i, q * layers + a - 1 if a > 0 else padded + side + q] = -1
        fixed[1, i, i] = -1
        fixed[1, i, i + 1 if a < layers - 1 else padded + r] = 1
        fixed[2, i, i] = -1
        fixed[2, i, i - 1 if a > 0 else padded + side + r] = 1
        for m in range(HB):
            fixed[0, i, (m * NV + v) * layers + a] = scale * harmonic[n, m]
    modes = np.zeros((up_to(walls_k * passages, 16), 2 * walls_k * passages), np.float32)
    for p in range(passages):
        for d in range(passages):
            angle = 2.0 * math.pi * (d * p % passages) / passages
            for k in range(walls_k):
                modes[p * walls_k + k, k * passages + d] = math.cos(angle)
                modes[p * walls_k + k, (walls_k + k) * passages + d] = -math.sin(angle)
    arrays = (
        mix.astype(BF16),
        axial.astype(BF16),
        fixed.reshape(3 * padded, width).astype(BF16),
        pick.astype(BF16),
        weights,
        of_row.astype(BF16),
        of_column.astype(BF16),
        modes,
    )
    return arrays, scale


def dot(a, b):
    return jnp.dot(a, b, preferred_element_type=F32)


def kernel(
    *refs, n_in, n_cell, n_circ, layers, padded, scale,
):
    sources = refs[:n_in]
    image, modal = refs[n_in : n_in + 2]
    held_in = refs[n_in + 2 : 2 * n_in + 2]
    (
        state, time_coef, axial_damp, plane_damp, periodic_damp, jac, faces, sides, face_map,
        wall_cells, normals, press_w, mode_shapes,
        mix_c, axial_c, fixed_c, pick_c, weights_c, of_row_c, of_column_c, modes_c,
    ) = held_in
    (
        extra, signed, joint, stack, cell_out, above, below, side_out, side_next, side_prev,
        forces, modes_high, modes_low, flux, total,
        cell_send, cell_recv, side_send, side_recv, force_send, force_recv, load_sem,
    ) = refs[2 * n_in + 2 :]
    me_cell = lax.axis_index("cell")
    me_circ = lax.axis_index("circ")
    me = me_circ * n_cell + me_cell

    def cell_at(j):
        return {"cell": lax.rem(me_cell + j, n_cell)}

    def circ_at(j):
        return {"circ": lax.rem(me_circ + j, n_circ)}

    def peer(i, j):
        return {"circ": lax.rem(me_circ + i, n_circ), "cell": lax.rem(me_cell + j, n_cell)}

    peers = [(i % n_circ, j) for i in range(1, n_circ + 1) for j in range(n_cell)][:-n_cell]
    peers += [(0, j) for j in range(1, n_cell)]
    loads = {}

    def fetch(which):
        for at in which:
            loads[at] = pltpu.make_async_copy(sources[at], held_in[at], load_sem.at[at])
            loads[at].start()

    fetch(LOAD_ORDER[:2])
    peers = [(i % n_circ, j) for i in range(1, n_circ + 1) for j in range(n_cell)][:-n_cell]
    peers += [(0, j) for j in range(1, n_cell)]
    barrier = pltpu.get_barrier_semaphore()
    for i, j in peers:
        pl.semaphore_signal(barrier, inc=1, device_id=peer(i, j), device_id_type=MESH)
    fetch(LOAD_ORDER[2:])

    def load(*which):
        for at in which:
            loads.pop(at).wait()

    n_rows, _, cells = state.shape
    n_faces = faces.shape[1]
    n_walls = wall_cells.shape[1]
    per = sides.shape[1]
    side_rows = above.shape[0]
    walls_k = normals.shape[0]
    groups = padded // 8

    def by_layer(value, pattern):
        return (value.reshape(groups, 8, value.shape[1]) * pattern[None]).reshape(value.shape)

    def pattern_of(rows):
        return jnp.concatenate([rows] * (8 // layers), axis=0)

    def remote(source, target, send_sem, recv_sem, device):
        return pltpu.make_async_remote_copy(
            src_ref=source, dst_ref=target, send_sem=send_sem, recv_sem=recv_sem,
            device_id=device, device_id_type=MESH,
        )

    to_below = remote(
        cell_out.at[pl.ds(0, side_rows)], above, cell_send.at[0], cell_recv.at[0],
        cell_at(n_cell - 1),
    )
    to_above = remote(
        cell_out.at[pl.ds(side_rows, side_rows)], below, cell_send.at[1], cell_recv.at[1],
        cell_at(1),
    )
    to_prev = remote(
        side_out.at[0], side_next, side_send.at[0], side_recv.at[0], circ_at(n_circ - 1)
    )
    to_next = remote(side_out.at[1], side_prev, side_send.at[1], side_recv.at[1], circ_at(1))
    has_below = me_cell > 0
    has_above = me_cell < n_cell - 1

    def send_sides():
        pl.when(has_above)(to_above.start)
        pl.when(has_below)(to_below.start)
        to_prev.start()
        to_next.start()

    band = lax.broadcasted_iota(jnp.int32, (GROUP, 128), 0).astype(F32).astype(BF16)
    one = jnp.ones((GROUP, 128), BF16)
    zero = jnp.zeros((GROUP, 128), BF16)

    def spread(row):
        return jnp.broadcast_to(row.astype(F32).astype(BF16), (GROUP, 128))

    def split(row):
        high = lax.shift_right_logical(row, GROUP.bit_length() - 1)
        return spread(high), jnp.where(band == spread(row - high * GROUP), one, zero)

    def mark(columns, first):
        for at in range(0, columns.shape[1], 128):
            high, low = split(columns[:, at : at + 128])
            for h in range(cells // GROUP):
                hit = jnp.where(high == h, low, zero)
                here = slice(first + at, first + at + 128)
                extra[h * GROUP : (h + 1) * GROUP, here] = hit.astype(F8)

    load(WALL_CELLS)
    wall_index = wall_cells[...]
    wall_layer = lax.div(wall_index, cells)
    mark(wall_index - wall_layer * cells, 0)

    load(STATE)
    wide = state[...].astype(F32)
    pieces = [wide[r] for r in range(n_rows)]
    pieces.append(jnp.zeros((padded - n_rows * layers, cells), F32))
    u = jnp.concatenate(pieces, axis=0).astype(BF16)
    stack[0:padded, :] = u

    load(NORMALS, PRESS_W, WEIGHTS_C)
    gathered = dot(u, extra[:, 0:n_walls])
    layer_of = lax.rem(lax.broadcasted_iota(jnp.int32, (8, n_walls), 0), layers)
    here = by_layer(gathered, (layer_of == wall_layer).astype(F32)).astype(BF16)
    weight_class = weights_c[...]
    weight = jnp.zeros(weight_class.shape, F32)
    for v in range(NV):
        weight = jnp.where(weight_class == v + 1, press_w[v], weight)
    high = weight.astype(BF16)
    low = (weight - high.astype(F32)).astype(BF16)
    pressure = dot(high, here) + dot(low, here)
    pitch, per_row, _ = force_slots(n_circ, walls_k)
    lane = lax.broadcasted_iota(jnp.int32, (8, 128), 1)
    lane = lane - lax.broadcasted_iota(jnp.int32, (8, 128), 0) - lax.rem(me_circ, per_row) * pitch
    tile = jnp.zeros((8, 128), F32)
    for k in range(walls_k):
        force = jnp.sum(pressure * normals[k : k + 1, :], axis=1, keepdims=True)
        tile = jnp.where(lane == k * 8, force, tile)
    forces[me] = jnp.sum(tile, axis=0, keepdims=True)

    early = me_circ < n_circ // 4
    late = me_circ >= n_circ // 4

    def enter():
        pl.semaphore_wait(barrier, n_cell * n_circ - 1)

    def send_forces():
        for i, j in peers:
            remote(forces.at[me], forces.at[me], force_send, force_recv, peer(i, j)).start()

    def enter_and_send_forces():
        enter()
        send_forces()

    def enter_and_send_all():
        enter()
        send_sides()
        send_forces()

    pl.when(late)(enter_and_send_forces)

    load(FACE_MAP, SIDES, PERIODIC_DAMP, AXIAL_DAMP, PICK_C)
    order = face_map[...]
    hits = (lax.broadcasted_iota(jnp.int32, (per, per), 0) == order).astype(F32)
    targets = jnp.dot(sides[0:1, :].astype(F32), hits, precision=HI, preferred_element_type=F32)
    targets = (targets + 0.5).astype(jnp.int32)
    mark(jnp.concatenate([sides[1:2, :], targets], axis=1), n_walls)

    own_side = dot(u, extra[:, n_walls:])
    side_damp = periodic_damp[0].astype(F32)
    side_pattern = pattern_of(jnp.concatenate([side_damp, side_damp], axis=1))
    half = padded // 2
    left = lax.broadcasted_iota(jnp.int32, (half, 2 * per), 1) < per
    first_half, second_half = own_side[0:half], own_side[half:]
    filler = [side_pattern] * ((side_out.shape[1] - half) // 8)
    lower_own = jnp.where(left, pltpu.roll(first_half, per, 1), second_half)
    upper_own = jnp.where(left, first_half, pltpu.roll(second_half, per, 1))
    side_out[0] = jnp.concatenate([lower_own, *filler], axis=0).astype(BF16)
    side_out[1] = jnp.concatenate([upper_own, *filler], axis=0).astype(BF16)

    damp = axial_damp[0].astype(F32)
    last = damp[layers - 1 : layers]
    picked = dot(pick_c[...], u)
    spare = lax.broadcasted_iota(jnp.int32, (16, cells), 0) == 15
    tail = jnp.where(spare, jnp.broadcast_to(last, (16, cells)), picked[2 * side_rows - 16 :])
    cell_out[0 : 2 * side_rows - 16, :] = picked[0 : 2 * side_rows - 16].astype(BF16)
    cell_out[2 * side_rows - 16 :, :] = tail.astype(BF16)

    pl.when(late)(send_sides)

    load(JAC, OF_ROW_C, OF_COLUMN_C, MIX_C, AXIAL_C, PLANE_DAMP, FACES)

    def mixing(face, mask):
        values = (0.5 * jac[:, face, :]).astype(BF16)
        across = dot(values, of_column_c[:, : mask.shape[1]]).astype(BF16)
        return (dot(of_row_c[...], across) * mask.astype(F32)).astype(BF16)

    axial_mix = mixing(0, axial_c[...])
    plane_mix = mixing(1, mix_c[...])
    side_mix = mixing(2, mix_c[...])

    convected = dot(plane_mix, u).astype(BF16)
    plane_pattern = pattern_of(0.5 * plane_damp[0].astype(F32))

    def build(first, count):
        for at in range(first, first + count, 128):
            owner_high, owner = split(faces[0:1, at : at + 128])
            other_high, other = split(faces[1:2, at : at + 128])
            same = owner_high == other_high
            both = owner - other
            by_owner = jnp.where(same, both, owner)
            by_other = jnp.where(same, both, -other)
            for h in range(cells // GROUP):
                hit = jnp.where(other_high == h, by_other, zero)
                hit = jnp.where(owner_high == h, by_owner, hit)
                here = slice(h * GROUP, (h + 1) * GROUP)
                signed[here, at : at + 128] = hit.astype(F8)
                joint[here, at : at + 128] = jnp.abs(hit).astype(F8)

    def gather(first, count):
        here = slice(first, first + count)
        damped = by_layer(dot(u, signed[:, here]), plane_pattern[:, here])
        flux[:, here] = (dot(convected, joint[:, here]) + damped).astype(BF16)

    part = 256
    starts = list(range(0, n_faces, part))
    build(0, part)
    for at in starts:
        if at + part < n_faces:
            build(at + part, part)
        gather(at, part)

    load(MODE_SHAPES, MODES_C)
    shapes = mode_shapes[...].reshape(2 * walls_k * n_circ, mode_shapes.shape[3])
    by_passage = jnp.dot(modes_c[...], shapes, precision=HI, preferred_element_type=F32)
    modes_high[...] = jnp.zeros(modes_high.shape, BF16)
    modes_low[...] = jnp.zeros(modes_low.shape, BF16)
    for p in range(n_circ):
        first = p // per_row * 128 + p % per_row * pitch
        rows = [by_passage[p * walls_k + k : p * walls_k + k + 1] for k in range(walls_k)]
        rows = [jnp.broadcast_to(row, (8, row.shape[1])) for row in rows]
        rows += [jnp.zeros_like(rows[0])] * (pitch // 8 - walls_k)
        rows = jnp.concatenate(rows, axis=0)
        high = rows.astype(BF16)
        modes_high[first : first + pitch, :] = high
        modes_low[first : first + pitch, :] = (rows - high.astype(F32)).astype(BF16)

    pl.when(early)(enter_and_send_all)

    total[...] = lax.dot_general(
        flux[...], signed[...], NT, preferred_element_type=F32
    )


    pl.when(has_above)(to_below.wait_recv)
    pl.when(has_below)(to_above.wait_recv)
    load(FIXED_C, TIME_COEF)
    above_rows = above[...].astype(F32)
    stack[padded : padded + side_rows, :] = jnp.where(
        me_cell == n_cell - 1, 0.0, above_rows
    ).astype(BF16)
    below_rows = below[...].astype(F32)
    stack[padded + side_rows :, :] = jnp.where(
        me_cell == 0, -cell_out[0:side_rows, :].astype(F32), below_rows
    ).astype(BF16)
    below_damp = below[side_rows - 16 : side_rows, :].astype(F32)[15:16]
    below_damp = jnp.where(me_cell == 0, 0.0, below_damp)
    held = stack[...]
    derived = dot(fixed_c[...], held)
    result = by_layer(derived[0:padded], pattern_of(time_coef[0] * (1.0 / scale)))
    result = result - by_layer(derived[padded : 2 * padded], pattern_of(0.5 * damp))
    lower_damp = jnp.concatenate([below_damp, damp[0 : layers - 1]], axis=0)
    result = result - by_layer(derived[2 * padded :], pattern_of(0.5 * lower_damp))
    result = result + dot(axial_mix, held)

    to_prev.wait_recv()
    to_next.wait_recv()
    ahead = side_next[0:half, :].astype(F32)
    back = side_prev[0:half, :].astype(F32)
    back_damp = side_prev[half:, :].astype(F32)[0:8]
    ahead = jnp.concatenate([ahead, pltpu.roll(ahead, per, 1)], axis=0)
    back = jnp.concatenate([pltpu.roll(back, per, 1), back], axis=0)
    left = jnp.concatenate([left, left], axis=0)
    lower = jnp.where(left, own_side, back)
    upper = jnp.where(left, ahead, own_side)
    side_s = 0.5 * jnp.where(left[0:8], side_pattern, back_damp)
    lower_b, upper_b = lower.astype(BF16), upper.astype(BF16)
    side_flux = dot(side_mix, lower_b) + dot(side_mix, upper_b)
    side_flux = side_flux - by_layer(upper - lower, side_s)
    side_flux = jnp.where(left, side_flux, -side_flux).astype(BF16)
    result = result + lax.dot_general(
        side_flux, extra[:, n_walls:], NT, preferred_element_type=F32
    )
    result = result + total[...]
    for r in range(n_rows):
        image[r] = result[r * layers : (r + 1) * layers].astype(BF16)

    others = n_cell * n_circ - 1
    arrived = pltpu.make_async_remote_copy(
        src_ref=forces.at[pl.ds(0, others)], dst_ref=forces.at[pl.ds(0, others)],
        send_sem=force_send, recv_sem=force_recv, device_id=peer(0, 1), device_id_type=MESH,
    )
    arrived.wait_recv()
    sublane = lax.broadcasted_iota(jnp.int32, (8, 128), 0)
    kept = lax.rem(lax.broadcasted_iota(jnp.int32, (8, 128), 1), 8) == sublane
    rows = []
    for first in range(0, n_circ, per_row):
        slots = range(first * n_cell, min(first + per_row, n_circ) * n_cell)
        row = [forces[slot] for slot in slots]
        while len(row) > 1:
            row = [a + b for a, b in zip(row[::2], row[1::2])] + row[len(row) // 2 * 2 :]
        rows.append(jnp.where(kept, jnp.broadcast_to(row[0], (8, 128)), 0.0))
    every = jnp.concatenate(rows, axis=1)
    high = every.astype(BF16)
    low = (every - high.astype(F32)).astype(BF16)
    table = modes_high[...]
    answer = dot(high, table) + dot(low, table) + dot(high, modes_low[...])
    modal[...] = answer[0:HB]
    arrived.wait_send()
    to_prev.wait_send()
    to_next.wait_send()
    pl.when(has_above)(to_above.wait_send)
    pl.when(has_below)(to_below.wait_send)


def deliver(image, modal, image_out, modal_out, sems):
    copies = [
        pltpu.make_async_copy(image, image_out, sems.at[0]),
        pltpu.make_async_copy(modal, modal_out, sems.at[1]),
    ]
    for copy in copies:
        copy.start()
    for copy in copies:
        copy.wait()


def shards(
    flow_state, time_coef, axial_damp, plane_damp, periodic_damp, flux_jacobian, face_cells,
    periodic_cells, face_map, wall_cells, wall_normals, pressure_weights, mode_shapes,
):
    layers, cells = flow_state.shape[2:]
    n_cell = lax.axis_size("cell")
    n_circ = lax.axis_size("circ")
    walls_k = wall_normals.shape[0]
    n_modes = mode_shapes.shape[3]
    per = face_map.shape[0]
    n_faces = face_cells.shape[1]
    n_walls = wall_cells.shape[0]
    fixed, scale = constants(layers, n_circ, walls_k)
    padded = fixed[0].shape[0]
    side = fixed[3].shape[0] // 2
    lanes = force_slots(n_circ, walls_k)[2]
    packed = up_to(padded // 2 + 8, 16)
    state = flow_state.reshape(HB * NV, layers, cells)
    vmem = pl.BlockSpec(memory_space=pltpu.VMEM)
    dma = pltpu.SemaphoreType.DMA
    operands = (
        state, time_coef, axial_damp, plane_damp, periodic_damp,
        flux_jacobian.transpose(1, 0, 2), face_cells, periodic_cells, face_map[None],
        wall_cells[None], wall_normals, pressure_weights,
        mode_shapes.transpose(0, 2, 1, 3), *(jnp.asarray(array) for array in fixed),
    )
    hbm = pl.BlockSpec(memory_space=pltpu.HBM)
    held = [
        (pltpu.SMEM if at == PRESS_W else pltpu.VMEM)(array.shape, array.dtype)
        for at, array in enumerate(operands)
    ]
    image, modal = pl.pallas_call(
        functools.partial(
            kernel, n_in=len(operands), n_cell=n_cell, n_circ=n_circ, layers=layers,
            padded=padded, scale=scale,
        ),
        out_shape=(
            jax.ShapeDtypeStruct((HB * NV, layers, cells), BF16),
            jax.ShapeDtypeStruct((HB, n_modes), F32),
        ),
        in_specs=[hbm] * len(operands),
        out_specs=(vmem, vmem),
        scratch_shapes=[
            *held,
            pltpu.VMEM((cells, n_walls + 2 * per), F8),
            pltpu.VMEM((cells, n_faces), F8),
            pltpu.VMEM((cells, n_faces), F8),
            pltpu.VMEM((padded + 2 * side, cells), BF16),
            pltpu.VMEM((2 * side, cells), BF16),
            pltpu.VMEM((side, cells), BF16),
            pltpu.VMEM((side, cells), BF16),
            pltpu.VMEM((2, packed, 2 * per), BF16),
            pltpu.VMEM((packed, 2 * per), BF16),
            pltpu.VMEM((packed, 2 * per), BF16),
            pltpu.VMEM((n_circ * n_cell, 1, 128), F32),
            pltpu.VMEM((lanes, n_modes), BF16),
            pltpu.VMEM((lanes, n_modes), BF16),
            pltpu.VMEM((padded, n_faces), BF16),
            pltpu.VMEM((padded, cells), F32),
            dma((2,)), dma((2,)), dma((2,)), dma((2,)), dma, dma, dma((len(operands),)),
        ],
        compiler_params=pltpu.CompilerParams(
            collective_id=0, has_side_effects=True, vmem_limit_bytes=VMEM_LIMIT
        ),
    )(*(pltpu.with_memory_space_constraint(array, pltpu.HBM) for array in operands))
    image, modal = pl.pallas_call(
        deliver,
        out_shape=(
            jax.ShapeDtypeStruct(image.shape, BF16),
            jax.ShapeDtypeStruct(modal.shape, F32),
        ),
        in_specs=[vmem] * 2,
        out_specs=(hbm, hbm),
        scratch_shapes=[dma((2,))],
        compiler_params=pltpu.CompilerParams(vmem_limit_bytes=VMEM_LIMIT),
    )(image, modal)
    return image.reshape(HB * NV, 1, layers, cells), modal


def solution(mesh):
    circ = P("circ", "cell", None)
    placed = (
        P(None, "circ", "cell", None), circ, circ, circ, circ, P(), P(), P(), P(),
        P("cell"), P(None, "cell"), P(), P(),
    )
    return jax.shard_map(
        shards,
        mesh=mesh,
        in_specs=placed,
        out_specs=(P(None, "circ", "cell", None), P()),
        check_vma=False,
    )
```
